512 devices in a mesh: expert: 32 (over z, y_lo), tensor: 16 (over y_hi, x, core).
Axes of the slice: x: 4, y: 4 (y_hi: 2, y_lo: 2; y = y_hi * 2 + y_lo), z: 16, core: 2. Of those that a mesh axis runs over, the one named last changes fastest.
Arguments:
- tokens: bfloat16 [8192, 2560], P('expert', 'tensor'), may hold values from -6 to 6
- route_logit: float32 [8192], P('expert'), may hold values from -6 to 6
- expert_ids: int32 [8192, 1], P('expert'), may hold values from 0 to 31; in each aligned block of 256 rows (0 to 255, 256 to 511, ...) at most 10 rows name the same one
- w_gate: bfloat16 [32, 2560, 4096], P('expert', None, 'tensor'), may hold values from -0.125 to 0.125
- w_up: bfloat16 [32, 2560, 4096], P('expert', None, 'tensor'), may hold values from -0.125 to 0.125
- w_down: bfloat16 [32, 4096, 2560], P('expert', 'tensor'), may hold values from -0.09375 to 0.09375
Outputs:
- mixed: bfloat16 [8192, 2560], P('expert', 'tensor')
The draws below stay inside these ranges and needn't reach their ends.
Inputs may be any that keep to these rules, and one draw needn't show every extreme that they name: `expert_ids`: in each aligned block of 256 tokens no expert id appears more than 10 times, and in some block one expert appears exactly 10 times.
All inputs are finite; a program needn't handle non-finite values.
Results may differ from the reference program's by a relative error of at most 0.0065.
Values may be sent and summed in bfloat16 or wider, within the bound.
No kernel may reach another device: no remote copies, remote signals or barrier semaphores. Data moves between devices by JAX's collectives and lax.ppermute only.
A program may use at most 64 MiB of HBM per device.

```python
import math
import jax
import jax.numpy as jnp
import numpy as np
from jax import lax

D = 2560
FF = 4096
TOK_G = 256
EXPERTS = 32
CAP = 10
TOKENS = 8192
N_EXPERT = 32


def block_scale(key, shape, pieces, low, high):
    def one(axis_at, blocks):
        heights = jax.random.uniform(jax.random.fold_in(jax.random.fold_in(key, 6), axis_at), (blocks,), jnp.float32, low / len(pieces), high / len(pieces))
        return jnp.repeat(jnp.exp(heights), shape[axis_at] // blocks).reshape((-1,) + (1,) * (len(shape) - axis_at - 1))

    loudness = one(*pieces[0])
    for cut in pieces[1:]:
        loudness = loudness * one(*cut)
    return loudness


def assign_block(stream_key, own, number, rows, amount, top, most, lean):
    ranking = jax.random.permutation(stream_key, amount)
    crowded, common = load_shares(amount, rows * top, most, lean, True), load_shares(amount, rows * top, most, lean, False)
    places = jnp.arange(amount)

    def named(tallies, offset_by):
        used = int((tallies > 0).sum())
        fixed = max(1, used // 4)
        shifted = fixed + (places - fixed + offset_by * (used - fixed)) % max(1, amount - fixed)
        return jnp.zeros((amount,), jnp.int32).at[ranking[jnp.where(places < fixed, places, shifted)]].set(jnp.asarray(tallies, jnp.int32))

    tallies = jnp.where(number % 4 == 0, named(crowded, number // 4), named(common, number - number // 4 - 1))
    mixed = jax.random.permutation(jax.random.fold_in(own, 3), amount)
    donor, sink = mixed[0:amount // 2 * 2:2], mixed[1:amount // 2 * 2:2]
    room = jnp.minimum(tallies[donor] - 1, most - tallies[sink]) // 2
    room = jnp.where((donor == ranking[0]) | (sink == ranking[0]) | (tallies[sink] == 0), 0, jnp.maximum(room, 0))
    shifted = jax.random.randint(jax.random.fold_in(own, 4), (amount // 2,), 0, 1 << 20) % (room + 1)
    tallies = tallies.at[donor].add(-shifted).at[sink].add(shifted)
    labels = jnp.searchsorted(jnp.cumsum(tallies), jnp.arange(rows * top), side="right").astype(jnp.int32)
    table = labels.reshape(top, rows).T
    table = table[jax.random.permutation(jax.random.fold_in(own, 1), rows)]
    offset_by = jax.random.randint(jax.random.fold_in(own, 2), (rows, 1), 0, top)
    return jnp.take_along_axis(table, (jnp.arange(top)[None, :] + offset_by) % top, axis=1)


def load_shares(amount, total, most, slope, full):
    loads = [(1 << 20) // math.isqrt(standing ** slope) + 1 for standing in range(1, amount + 1)]
    largest = most if full else min(most, max(-(-total // amount), total * loads[0] // sum(loads)))
    least = 1 if total - largest >= amount - 1 else 0
    given, spare = [largest] + [least] * (amount - 1), total - largest - least * (amount - 1)
    while spare > 0:
        candidates = [i for i in range(1, amount) if given[i] < largest] or [i for i in range(1, amount) if given[i] < most]
        whole, remaining = sum([loads[i] for i in candidates]), spare
        for i in candidates:
            extra = min(most - given[i], max(1, remaining * loads[i] // whole), spare)
            given[i] = given[i] + extra
            spare = spare - extra
    return np.array(given)


def bell_draw(key, extent, scale, most, cuts=(), kind=jnp.bfloat16):
    entries = jax.random.normal(key, extent, jnp.float32) * scale
    if len(cuts) > 0:
        entries = block_scale(key, extent, cuts, -0.22, 0.18) * entries
    return jnp.clip(entries, min=-most, max=most).astype(kind)


def setup_inputs(seed: int = 0) -> dict:
    streams_of = jax.random.split(jax.random.key(seed), 7)
    tokens = bell_draw(streams_of[0], (TOKENS, D), 1.0, 6.0, ((0, 32), (1, 16)))
    route_logit = bell_draw(streams_of[1], (TOKENS,), 1.5, 6.0, ((0, 32),), jnp.float32)
    expert_ids_keys = jax.random.split(jax.random.fold_in(streams_of[2], 1), TOKENS // TOK_G)
    expert_ids_turns = jax.random.permutation(jax.random.fold_in(streams_of[2], 3), TOKENS // TOK_G)
    expert_ids = jax.vmap(lambda own, number: assign_block(jax.random.fold_in(streams_of[2], 2), own, number, TOK_G, EXPERTS, 1, CAP, 2))(expert_ids_keys, expert_ids_turns).reshape((TOKENS, 1))
    w_gate = bell_draw(streams_of[3], (EXPERTS, D, FF), D ** -0.5, 0.125, ((0, 32), (2, 16)))
    w_up = bell_draw(streams_of[4], (EXPERTS, D, FF), D ** -0.5, 0.125, ((0, 32), (2, 16)))
    w_down = bell_draw(streams_of[5], (EXPERTS, FF, D), FF ** -0.5, 0.09375, ((0, 32), (1, 16)))
    return dict(tokens=tokens, route_logit=route_logit, expert_ids=expert_ids, w_gate=w_gate, w_up=w_up, w_down=w_down)


def expert_ffn(items):
    rows, gate_w, up_w, down_w = items
    rows_f = rows.astype(jnp.float32)
    gate_val = jnp.dot(rows_f, gate_w.astype(jnp.float32), precision=lax.Precision.HIGHEST)
    lift_val = jnp.dot(rows_f, up_w.astype(jnp.float32), precision=lax.Precision.HIGHEST)
    hidden = (jax.nn.silu(gate_val) * lift_val).astype(jnp.bfloat16)
    result = jnp.dot(hidden.astype(jnp.float32), down_w.astype(jnp.float32), precision=lax.Precision.HIGHEST)
    return result.astype(jnp.bfloat16)


def reference(tokens, route_logit, expert_ids, w_gate, w_up, w_down):
    route = expert_ids[:, 0].astype(jnp.int32)
    factor = jax.nn.sigmoid(route_logit.astype(jnp.float32))
    scaled = (factor[:, None] * tokens.astype(jnp.float32)).astype(jnp.bfloat16)
    one_hot = (route[:, None] == jnp.arange(EXPERTS, dtype=jnp.int32)[None, :]).astype(jnp.int32)
    blocked = one_hot.reshape(N_EXPERT, TOK_G, EXPERTS)
    earlier = jnp.cumsum(blocked, axis=1) - blocked
    position = jnp.sum(earlier * blocked, axis=2).reshape(TOKENS).astype(jnp.int32)
    block_index = (jnp.arange(TOKENS, dtype=jnp.int32) // TOK_G).astype(jnp.int32)
    row_index = (block_index * CAP + position).astype(jnp.int32)
    buffer = jnp.zeros((EXPERTS, N_EXPERT * CAP, D), jnp.bfloat16).at[route, row_index].set(scaled)
    outputs = lax.map(expert_ffn, (buffer, w_gate, w_up, w_down))
    return outputs[route, row_index]
```

```python
import jax
import jax.numpy as jnp
from jax import lax
from jax.sharding import Mesh, PartitionSpec as P

EXPERT = ("z", "yl")
TENSOR = ("yh", "x", "core")


def on_device(tokens, route_logit, expert_ids, w_gate, w_up, w_down):
    experts = lax.axis_size(EXPERT)
    parts = lax.axis_size(TENSOR)
    chips = parts // 2
    tok_rows, width = tokens.shape
    capacity = 5 * tok_rows // (4 * experts)
    half = capacity // 2
    slots = experts * capacity
    rows = experts * half
    swap = [(0, 1), (1, 0)]
    other_in = lax.ppermute(jnp.concatenate([w_gate[0], w_up[0]], axis=1), "core", swap)
    other_down = lax.ppermute(w_down[0], "core", swap)

    route = expert_ids[:, 0]
    one_hot = (route[:, None] == jnp.arange(experts, dtype=jnp.int32)[None, :]).astype(jnp.bfloat16)
    before = (jnp.arange(tok_rows)[:, None] > jnp.arange(tok_rows)[None, :]).astype(jnp.bfloat16)
    earlier = jnp.dot(before, one_hot, preferred_element_type=jnp.float32)
    position = jnp.sum(earlier * one_hot.astype(jnp.float32), axis=1).astype(jnp.int32)
    destination = route * capacity + position
    dispatch_map = (
        jnp.arange(slots, dtype=jnp.int32)[:, None] == destination[None, :]
    ).astype(jnp.bfloat16)
    factor = jax.nn.sigmoid(route_logit)
    scaled = (factor[:, None] * tokens.astype(jnp.float32)).astype(jnp.bfloat16)
    outgoing = jnp.dot(dispatch_map, scaled, preferred_element_type=jnp.float32).astype(jnp.bfloat16)
    arrived = lax.all_to_all(
        outgoing.reshape(experts, capacity, width), EXPERT, 0, 0, tiled=True
    )
    halves = arrived.reshape(experts, 2, half, width).transpose(1, 0, 2, 3)
    packed = halves.reshape(2, rows * width // 128, 128)
    packed = jnp.broadcast_to(packed[None], (chips,) + packed.shape).reshape(parts, -1, 128)
    piece = lax.all_to_all(packed, TENSOR, 0, 0, tiled=True)
    piece = piece.reshape(parts, rows, width).transpose(1, 0, 2).reshape(rows, parts * width)

    weights = jnp.concatenate([w_gate[0], w_up[0]], axis=1)
    own = jnp.dot(piece, weights, preferred_element_type=jnp.float32)
    sib = jnp.dot(piece, other_in, preferred_element_type=jnp.float32)
    ff = w_gate.shape[2]
    hid_own = (jax.nn.silu(own[:, :ff]) * own[:, ff:]).astype(jnp.bfloat16)
    hid_sib = (jax.nn.silu(sib[:, :ff]) * sib[:, ff:]).astype(jnp.bfloat16)
    partial = jnp.dot(hid_own, w_down[0], preferred_element_type=jnp.float32) + jnp.dot(
        hid_sib, other_down, preferred_element_type=jnp.float32
    )
    partial = partial.astype(jnp.bfloat16).reshape(rows, parts, width).transpose(1, 0, 2)
    partial = partial.reshape(parts, rows * width // 128, 128)
    terms = lax.all_to_all(partial, TENSOR, 0, 0, tiled=True)
    terms = terms.reshape(chips, 2, -1, 128)
    summed = jnp.sum(terms.astype(jnp.float32), axis=0).astype(jnp.bfloat16)
    back = summed.reshape(2, experts, half, width).transpose(1, 0, 2, 3)
    returned = lax.all_to_all(
        back.reshape(experts, capacity, width), EXPERT, 0, 0, tiled=True
    ).reshape(slots, width)
    mixed = lax.dot_general(
        dispatch_map, returned, (((0,), (0,)), ((), ())), preferred_element_type=jnp.float32
    )
    return mixed.astype(jnp.bfloat16)


def solution(mesh):
    fine = Mesh(mesh.devices.reshape(16, 2, 2, 4, 2), EXPERT + TENSOR)
    return jax.shard_map(
        on_device,
        mesh=fine,
        in_specs=(
            P(EXPERT, TENSOR),
            P(EXPERT),
            P(EXPERT, None),
            P(EXPERT, None, TENSOR),
            P(EXPERT, None, TENSOR),
            P(EXPERT, TENSOR, None),
        ),
        out_specs=P(EXPERT, TENSOR),
        check_vma=False,
    )
```

```python
import jax
import jax.numpy as jnp
from jax import lax
from jax.experimental import pallas as pl
from jax.experimental.pallas import tpu as pltpu
from jax.sharding import Mesh, PartitionSpec as P

EXPERT = ("z", "yl")
TENSOR = ("yh", "x", "core")
BF16, F32, I32 = jnp.bfloat16, jnp.float32, jnp.int32

N_EXPERT, N_PART, N_CHIP = 32, 16, 8
TOK, WIDTH, FF = 256, 160, 256
MODEL = N_PART * WIDTH
HALF = 5
ROWS = N_EXPERT * HALF
LANES, TAIL = 128, WIDTH - 128
BLOCK = ROWS + N_EXPERT + 8
MSG = 16


def iota(shape, axis):
    return lax.broadcasted_iota(I32, shape, axis)


def slot_rows(ids):
    one_hot = (iota((N_EXPERT, TOK), 0) == ids).astype(F32)
    before = (iota((TOK, TOK), 0) < iota((TOK, TOK), 1)).astype(F32).astype(BF16)
    earlier = jnp.dot(one_hot.astype(BF16), before, preferred_element_type=F32)
    position = jnp.sum(earlier * one_hot, axis=0, keepdims=True).astype(I32)
    second = position >= HALF
    place = jnp.where(second, position - HALF, position)
    base = ids * MSG + jnp.where(second, 8, 0)
    last = place == HALF - 1
    group = jnp.where(last, lax.axis_index("z") // 4, place)
    return base + place, base + jnp.where(last, 6, 5), group


def slot_map(row_main, row_tail):
    at = iota((N_EXPERT * MSG, TOK), 0)
    main = (at == row_main).astype(F32).astype(BF16)
    tail = (at == row_tail).astype(F32).astype(BF16)
    return jnp.concatenate([main, tail], axis=1)


def dispatch_kernel(tok_ref, logit_ref, ids_ref, out_ref, aux_ref):
    row_main, row_tail, group = slot_rows(ids_ref[...])
    aux_ref[0:1, :] = row_main
    aux_ref[1:2, :] = row_tail
    aux_ref[2:3, :] = group
    aux_ref[3:8, :] = jnp.zeros((5, TOK), I32)
    factor = jax.nn.sigmoid(logit_ref[...])
    scaled = (tok_ref[...].astype(F32) * factor).astype(BF16)
    tails = jnp.concatenate([scaled[LANES:, :].astype(F32)] * 4, axis=0)
    tails = jnp.where(iota((LANES, TOK), 0) // TAIL == group, tails, 0.0).astype(BF16)
    both = jnp.concatenate([scaled[:LANES, :], tails], axis=1)
    out = lax.dot_general(
        slot_map(row_main, row_tail), both, (((1,), (1,)), ((), ())), preferred_element_type=F32
    )
    out_ref[...] = out.astype(BF16).reshape(N_EXPERT, MSG, LANES)


def weights_kernel(gate_ref, up_ref, down_ref, out_ref):
    for m in range(N_PART):
        src, dst = slice(WIDTH * m, WIDTH * m + LANES), slice(LANES * m, LANES * m + LANES)
        out_ref[dst, 0:FF] = gate_ref[0, src, :]
        out_ref[dst, FF : 2 * FF] = up_ref[0, src, :]
        src = slice(WIDTH * m + LANES, WIDTH * (m + 1))
        first = N_PART * LANES + TAIL * m
        dst = slice(first, first + TAIL)
        out_ref[dst, 0:FF] = gate_ref[0, src, :]
        out_ref[dst, FF : 2 * FF] = up_ref[0, src, :]
        k = m % 4
        at = WIDTH * m - TAIL * k
        window = down_ref[0, :, at : at + LANES]
        if k:
            low = down_ref[0, :, at + LANES : at + 2 * LANES].astype(F32)
            mixed = jnp.where(iota((FF, LANES), 1) >= TAIL * k, window.astype(F32), low)
            window = pltpu.roll(mixed, LANES - TAIL * k, 1).astype(BF16)
        rows, cols = FF * (m // 2), 2 * FF + LANES * (m % 2)
        out_ref[rows : rows + FF, cols : cols + LANES] = window
    for g in range(4):
        lanes = iota((FF, LANES), 1) // TAIL
        total = jnp.zeros((FF, LANES), F32)
        for k in range(4):
            at = 4 * WIDTH * g + LANES * (k + 1)
            total = jnp.where(lanes == k, down_ref[0, :, at : at + LANES].astype(F32), total)
        rows, cols = FF * (8 + g // 2), 2 * FF + LANES * (g % 2)
        out_ref[rows : rows + FF, cols : cols + LANES] = total.astype(BF16)


def spread_kernel(in_ref, out_ref):
    flat = in_ref[...].reshape(N_EXPERT * MSG, LANES)
    row, col = iota((BLOCK, N_EXPERT * MSG), 0), iota((BLOCK, N_EXPERT * MSG), 1)
    src, q = col // MSG, col % MSG
    for h in range(2):
        want_main = (row == (q - 8 * h) * N_EXPERT + src) & (q >= 8 * h) & (q < 8 * h + HALF)
        want_tail = (row == ROWS + src) & (q == 8 * h + 5)
        want_last = (row == ROWS + N_EXPERT + src % 8) & (q == 8 * h + 6)
        move = (want_main | want_tail | want_last).astype(F32).astype(BF16)
        block = jnp.dot(move, flat, preferred_element_type=F32).astype(BF16)
        for chip in range(N_CHIP):
            out_ref[2 * chip + h] = block


def expert_kernel(x_ref, own_ref, other_ref, out_ref, x_all, tails):
    lanes = iota((N_EXPERT, LANES), 1) // TAIL
    for m in range(N_PART):
        x_all[:, LANES * m : LANES * (m + 1)] = x_ref[m, 0:ROWS, :]
    for g in range(4):
        packed = [x_ref[4 * g + k, ROWS : ROWS + N_EXPERT, :].astype(F32) for k in range(4)]
        ends = [x_ref[4 * g + k, ROWS + N_EXPERT : BLOCK, :].astype(F32) for k in range(4)]
        cols = slice(N_PART * LANES + LANES * g, N_PART * LANES + LANES * (g + 1))
        last = []
        for p in range(4):
            total, end = jnp.zeros((N_EXPERT, LANES), F32), jnp.zeros((8, LANES), F32)
            for k in range(4):
                shift = (TAIL * (k - p)) % LANES
                a = pltpu.roll(packed[k], shift, 1) if shift else packed[k]
                b = pltpu.roll(ends[k], shift, 1) if shift else ends[k]
                total = jnp.where(lanes == k, a, total)
                end = jnp.where(lanes[0:8] == k, b, end)
            x_all[N_EXPERT * p : N_EXPERT * (p + 1), cols] = total.astype(BF16)
            last.append(end)
        x_all[4 * N_EXPERT : ROWS, cols] = jnp.concatenate(last, axis=0).astype(BF16)
    hidden = []
    for w_ref in (own_ref, other_ref):
        gate = jnp.dot(x_all[...], w_ref[:, 0:FF], preferred_element_type=F32)
        up = jnp.dot(x_all[...], w_ref[:, FF : 2 * FF], preferred_element_type=F32)
        hidden.append((gate / (1.0 + jnp.exp(-gate)) * up).astype(BF16))
    for i in range(10):
        part = sum(
            jnp.dot(h, w_ref[FF * i : FF * (i + 1), 2 * FF :], preferred_element_type=F32)
            for h, w_ref in zip(hidden, (own_ref, other_ref))
        )
        if i < 8:
            out_ref[2 * i, 0:ROWS, :] = part[:, 0:LANES].astype(BF16)
            out_ref[2 * i + 1, 0:ROWS, :] = part[:, LANES:].astype(BF16)
        else:
            tails[:, FF * (i - 8) : FF * (i - 7)] = part
    for g in range(4):
        cols = slice(LANES * g, LANES * (g + 1))
        for k in range(4):
            total, end = jnp.zeros((N_EXPERT, LANES), F32), jnp.zeros((8, LANES), F32)
            for p in range(4):
                shift = (TAIL * (p - k)) % LANES
                a = tails[N_EXPERT * p : N_EXPERT * (p + 1), cols]
                b = tails[4 * N_EXPERT + 8 * p : 4 * N_EXPERT + 8 * (p + 1), cols]
                a = pltpu.roll(a, shift, 1) if shift else a
                b = pltpu.roll(b, shift, 1) if shift else b
                total = jnp.where(lanes == p, a, total)
                end = jnp.where(lanes[0:8] == p, b, end)
            rest = jnp.concatenate([total, end], axis=0).astype(BF16)
            out_ref[4 * g + k, ROWS:BLOCK, :] = rest


def reduce_kernel(in_ref, out_ref):
    row, col = iota((N_EXPERT * MSG, BLOCK), 0), iota((N_EXPERT * MSG, BLOCK), 1)
    dst, q = row // MSG, row % MSG
    moved = jnp.zeros((N_EXPERT * MSG, LANES), F32)
    for h in range(2):
        total = in_ref[h].astype(F32)
        for chip in range(1, N_CHIP):
            total = total + in_ref[2 * chip + h].astype(F32)
        want_main = (col == (q - 8 * h) * N_EXPERT + dst) & (q >= 8 * h) & (q < 8 * h + HALF)
        want_tail = (col == ROWS + dst) & (q == 8 * h + 5)
        want_last = (col == ROWS + N_EXPERT + dst % 8) & (q == 8 * h + 6)
        move = (want_main | want_tail | want_last).astype(F32).astype(BF16)
        moved = moved + jnp.dot(move, total.astype(BF16), preferred_element_type=F32)
    out_ref[...] = moved.astype(BF16).reshape(N_EXPERT, MSG, LANES)


def combine_kernel(in_ref, aux_ref, out_ref):
    row_main, row_tail, group = aux_ref[0:1, :], aux_ref[1:2, :], aux_ref[2:3, :]
    flat = in_ref[...].reshape(N_EXPERT * MSG, LANES)
    got = lax.dot_general(
        flat, slot_map(row_main, row_tail), (((0,), (0,)), ((), ())), preferred_element_type=F32
    )
    out_ref[0:LANES, :] = got[:, :TOK].astype(BF16)
    tails = jnp.where(iota((LANES, TOK), 0) // TAIL == group, got[:, TOK:], 0.0)
    tail = tails[0:TAIL] + tails[TAIL : 2 * TAIL] + tails[2 * TAIL : 3 * TAIL] + tails[3 * TAIL :]
    out_ref[LANES:WIDTH, :] = tail.astype(BF16)


def call(kernel, name, out, args, mib=16, scratch=(), flops=0, moved=1 << 20):
    return pl.pallas_call(
        kernel,
        out_shape=out,
        scratch_shapes=list(scratch),
        compiler_params=pltpu.CompilerParams(vmem_limit_bytes=mib << 20),
        cost_estimate=pl.CostEstimate(flops=flops, bytes_accessed=moved, transcendentals=0),
        name=name,
    )(*args)


def exchange(x, axes):
    return lax.all_to_all(x, axes, 0, 0, tiled=True)


def on_device(tokens, route_logit, expert_ids, w_gate, w_up, w_down):
    shape = jax.ShapeDtypeStruct
    message = shape((N_EXPERT, MSG, LANES), BF16)
    blocks = shape((N_PART, BLOCK, LANES), BF16)
    sent, aux = call(
        dispatch_kernel, "dispatch", (message, shape((8, TOK), I32)),
        (tokens.T, route_logit.reshape(1, TOK), expert_ids.reshape(1, TOK)),
    )
    sent, w_gate, w_up, w_down = lax.optimization_barrier((sent, w_gate, w_up, w_down))
    arrived = exchange(sent, EXPERT)
    own = call(
        weights_kernel, "weights", shape((MODEL, 3 * FF), BF16), (w_gate, w_up, w_down),
        mib=32, moved=8 << 20,
    )
    other = lax.ppermute(own, "core", [(0, 1), (1, 0)])
    pieces = exchange(call(spread_kernel, "spread", blocks, (arrived,)), TENSOR)
    partial = call(
        expert_kernel, "expert", blocks, (pieces, own, other), mib=32,
        scratch=(pltpu.VMEM((ROWS, MODEL), BF16), pltpu.VMEM((ROWS, 4 * LANES), F32)),
        flops=12 * ROWS * MODEL * FF, moved=8 << 20,
    )
    terms = exchange(partial, TENSOR)
    back = call(reduce_kernel, "reduce", message, (terms,))
    returned = exchange(back, EXPERT)
    mixed = call(combine_kernel, "combine", shape((WIDTH, TOK), BF16), (returned, aux))
    return mixed.T


def solution(mesh):
    fine = Mesh(mesh.devices.reshape(16, 2, 2, 4, 2), EXPERT + TENSOR)
    return jax.shard_map(
        on_device,
        mesh=fine,
        in_specs=(
            P(EXPERT, TENSOR),
            P(EXPERT),
            P(EXPERT, None),
            P(EXPERT, None, TENSOR),
            P(EXPERT, None, TENSOR),
            P(EXPERT, TENSOR, None),
        ),
        out_specs=P(EXPERT, TENSOR),
        check_vma=False,
    )
```

```python
import jax
import jax.numpy as jnp
from jax import lax
from jax.experimental import pallas as pl
from jax.experimental.pallas import tpu as pltpu
from jax.sharding import Mesh, PartitionSpec as P

EXPERT = ("z", "yl")
TENSOR = ("yh", "x", "core")
BF16, F32, I32 = jnp.bfloat16, jnp.float32, jnp.int32

N_EXPERT, N_PART, N_CHIP = 32, 16, 8
TOK, WIDTH, FF = 256, 160, 256
MODEL = N_PART * WIDTH
HALF = 5
ROWS = N_EXPERT * HALF
LANES, TAIL = 128, WIDTH - 128
BLOCK = ROWS + N_EXPERT + 8
MSG = 16


def iota(shape, axis):
    return lax.broadcasted_iota(I32, shape, axis)


def slot_rows(ids):
    one_hot = (iota((N_EXPERT, TOK), 0) == ids).astype(F32)
    before = (iota((TOK, TOK), 0) < iota((TOK, TOK), 1)).astype(F32).astype(BF16)
    earlier = jnp.dot(one_hot.astype(BF16), before, preferred_element_type=F32)
    position = jnp.sum(earlier * one_hot, axis=0, keepdims=True).astype(I32)
    second = position >= HALF
    place = jnp.where(second, position - HALF, position)
    base = ids * MSG + jnp.where(second, 8, 0)
    last = place == HALF - 1
    group = jnp.where(last, lax.axis_index("z") // 4, place)
    return base + place, base + jnp.where(last, 6, 5), group


def slot_map(row_main, row_tail):
    at = iota((N_EXPERT * MSG, TOK), 0)
    main = (at == row_main).astype(F32).astype(BF16)
    tail = (at == row_tail).astype(F32).astype(BF16)
    return jnp.concatenate([main, tail], axis=1)


def dispatch_kernel(tok_hbm, logit_hbm, ids_hbm, out_ref, aux_ref, tok_ref, logit_ref, ids_ref, sems):
    copies = [
        pltpu.make_async_copy(src, dst, sems.at[i])
        for i, (src, dst) in enumerate(
            ((ids_hbm, ids_ref), (logit_hbm, logit_ref), (tok_hbm, tok_ref))
        )
    ]
    for copy in copies:
        copy.start()
    copies[0].wait()
    row_main, row_tail, group = slot_rows(ids_ref[...])
    aux_ref[0:1, :] = row_main
    aux_ref[1:2, :] = row_tail
    aux_ref[2:3, :] = group
    aux_ref[3:8, :] = jnp.zeros((5, TOK), I32)
    copies[1].wait()
    copies[2].wait()
    factor = jax.nn.sigmoid(logit_ref[...])
    scaled = (tok_ref[...].astype(F32) * factor).astype(BF16)
    tails = jnp.concatenate([scaled[LANES:, :].astype(F32)] * 4, axis=0)
    tails = jnp.where(iota((LANES, TOK), 0) // TAIL == group, tails, 0.0).astype(BF16)
    both = jnp.concatenate([scaled[:LANES, :], tails], axis=1)
    out = lax.dot_general(
        slot_map(row_main, row_tail), both, (((1,), (1,)), ((), ())), preferred_element_type=F32
    )
    out_ref[...] = out.astype(BF16).reshape(N_EXPERT, MSG, LANES)


def weights_kernel(gate_hbm, up_hbm, down_hbm, out_ref, down_ref, sems):
    down_copy = pltpu.make_async_copy(down_hbm, down_ref, sems.at[4 * N_PART])
    down_copy.start()
    copies = []
    for m in range(N_PART):
        main, tail = LANES * m, N_PART * LANES + TAIL * m
        for size, src, dst in ((LANES, WIDTH * m, main), (TAIL, WIDTH * m + LANES, tail)):
            for i, hbm in enumerate((gate_hbm, up_hbm)):
                target = out_ref.at[pl.ds(dst, size), pl.ds(FF * i, FF)]
                part = hbm.at[0, pl.ds(src, size)]
                copies.append(pltpu.make_async_copy(part, target, sems.at[len(copies)]))
                copies[-1].start()
    down_copy.wait()
    for m in range(N_PART):
        k = m % 4
        at = WIDTH * m - TAIL * k
        window = down_ref[0, :, at : at + LANES]
        if k:
            low = down_ref[0, :, at + LANES : at + 2 * LANES].astype(F32)
            mixed = jnp.where(iota((FF, LANES), 1) >= TAIL * k, window.astype(F32), low)
            window = pltpu.roll(mixed, LANES - TAIL * k, 1).astype(BF16)
        rows, cols = FF * (m // 2), 2 * FF + LANES * (m % 2)
        out_ref[rows : rows + FF, cols : cols + LANES] = window
    for g in range(4):
        lanes = iota((FF, LANES), 1) // TAIL
        total = jnp.zeros((FF, LANES), F32)
        for k in range(4):
            at = 4 * WIDTH * g + LANES * (k + 1)
            total = jnp.where(lanes == k, down_ref[0, :, at : at + LANES].astype(F32), total)
        rows, cols = FF * (8 + g // 2), 2 * FF + LANES * (g % 2)
        out_ref[rows : rows + FF, cols : cols + LANES] = total.astype(BF16)
    for copy in copies:
        copy.wait()


def spread_kernel(in_ref, out_ref):
    flat = in_ref[...].reshape(N_EXPERT * MSG, LANES)
    row, col = iota((BLOCK, N_EXPERT * MSG), 0), iota((BLOCK, N_EXPERT * MSG), 1)
    src, q = col // MSG, col % MSG
    for h in range(2):
        want_main = (row == (q - 8 * h) * N_EXPERT + src) & (q >= 8 * h) & (q < 8 * h + HALF)
        want_tail = (row == ROWS + src) & (q == 8 * h + 5)
        want_last = (row == ROWS + N_EXPERT + src % 8) & (q == 8 * h + 6)
        move = (want_main | want_tail | want_last).astype(F32).astype(BF16)
        block = jnp.dot(move, flat, preferred_element_type=F32).astype(BF16)
        for chip in range(N_CHIP):
            out_ref[2 * chip + h] = block


def hidden_units(x, w_ref):
    gate = jnp.dot(x, w_ref[:, 0:FF], preferred_element_type=F32)
    up = jnp.dot(x, w_ref[:, FF : 2 * FF], preferred_element_type=F32)
    return (gate / (1.0 + jnp.exp(-gate)) * up).astype(BF16)


def own_kernel(x_ref, own_ref, x_all, hidden_ref):
    lanes = iota((N_EXPERT, LANES), 1) // TAIL
    for m in range(N_PART):
        x_all[:, LANES * m : LANES * (m + 1)] = x_ref[m, 0:ROWS, :]
    for g in range(4):
        packed = [x_ref[4 * g + k, ROWS : ROWS + N_EXPERT, :].astype(F32) for k in range(4)]
        ends = [x_ref[4 * g + k, ROWS + N_EXPERT : BLOCK, :].astype(F32) for k in range(4)]
        cols = slice(N_PART * LANES + LANES * g, N_PART * LANES + LANES * (g + 1))
        last = []
        for p in range(4):
            total, end = jnp.zeros((N_EXPERT, LANES), F32), jnp.zeros((8, LANES), F32)
            for k in range(4):
                shift = (TAIL * (k - p)) % LANES
                a = pltpu.roll(packed[k], shift, 1) if shift else packed[k]
                b = pltpu.roll(ends[k], shift, 1) if shift else ends[k]
                total = jnp.where(lanes == k, a, total)
                end = jnp.where(lanes[0:8] == k, b, end)
            x_all[N_EXPERT * p : N_EXPERT * (p + 1), cols] = total.astype(BF16)
            last.append(end)
        x_all[4 * N_EXPERT : ROWS, cols] = jnp.concatenate(last, axis=0).astype(BF16)
    hidden_ref[...] = hidden_units(x_all[...], own_ref)


def expert_kernel(x_ref, hidden_ref, own_ref, other_ref, out_ref, tails):
    lanes = iota((N_EXPERT, LANES), 1) // TAIL
    hidden = (hidden_ref[...], hidden_units(x_ref[...], other_ref))
    for i in range(10):
        part = sum(
            jnp.dot(h, w_ref[FF * i : FF * (i + 1), 2 * FF :], preferred_element_type=F32)
            for h, w_ref in zip(hidden, (own_ref, other_ref))
        )
        if i < 8:
            out_ref[2 * i, 0:ROWS, :] = part[:, 0:LANES].astype(BF16)
            out_ref[2 * i + 1, 0:ROWS, :] = part[:, LANES:].astype(BF16)
        else:
            tails[:, FF * (i - 8) : FF * (i - 7)] = part
    for g in range(4):
        cols = slice(LANES * g, LANES * (g + 1))
        for k in range(4):
            total, end = jnp.zeros((N_EXPERT, LANES), F32), jnp.zeros((8, LANES), F32)
            for p in range(4):
                shift = (TAIL * (p - k)) % LANES
                a = tails[N_EXPERT * p : N_EXPERT * (p + 1), cols]
                b = tails[4 * N_EXPERT + 8 * p : 4 * N_EXPERT + 8 * (p + 1), cols]
                a = pltpu.roll(a, shift, 1) if shift else a
                b = pltpu.roll(b, shift, 1) if shift else b
                total = jnp.where(lanes == p, a, total)
                end = jnp.where(lanes[0:8] == p, b, end)
            rest = jnp.concatenate([total, end], axis=0).astype(BF16)
            out_ref[4 * g + k, ROWS:BLOCK, :] = rest


def reduce_kernel(in_ref, out_ref):
    row, col = iota((N_EXPERT * MSG, BLOCK), 0), iota((N_EXPERT * MSG, BLOCK), 1)
    dst, q = row // MSG, row % MSG
    moved = jnp.zeros((N_EXPERT * MSG, LANES), F32)
    for h in range(2):
        total = in_ref[h].astype(F32)
        for chip in range(1, N_CHIP):
            total = total + in_ref[2 * chip + h].astype(F32)
        want_main = (col == (q - 8 * h) * N_EXPERT + dst) & (q >= 8 * h) & (q < 8 * h + HALF)
        want_tail = (col == ROWS + dst) & (q == 8 * h + 5)
        want_last = (col == ROWS + N_EXPERT + dst % 8) & (q == 8 * h + 6)
        move = (want_main | want_tail | want_last).astype(F32).astype(BF16)
        moved = moved + jnp.dot(move, total.astype(BF16), preferred_element_type=F32)
    out_ref[...] = moved.astype(BF16).reshape(N_EXPERT, MSG, LANES)


def combine_kernel(in_ref, aux_ref, out_ref):
    row_main, row_tail, group = aux_ref[0:1, :], aux_ref[1:2, :], aux_ref[2:3, :]
    flat = in_ref[...].reshape(N_EXPERT * MSG, LANES)
    got = lax.dot_general(
        flat, slot_map(row_main, row_tail), (((0,), (0,)), ((), ())), preferred_element_type=F32
    )
    out_ref[0:LANES, :] = got[:, :TOK].astype(BF16)
    tails = jnp.where(iota((LANES, TOK), 0) // TAIL == group, got[:, TOK:], 0.0)
    tail = tails[0:TAIL] + tails[TAIL : 2 * TAIL] + tails[2 * TAIL : 3 * TAIL] + tails[3 * TAIL :]
    out_ref[LANES:WIDTH, :] = tail.astype(BF16)


def call(kernel, name, out, args, mib=16, scratch=(), flops=0, moved=1 << 20, space=pltpu.VMEM):
    if space is pltpu.HBM:
        args = [pltpu.with_memory_space_constraint(x, space) for x in args]
    return pl.pallas_call(
        kernel,
        out_shape=out,
        in_specs=[pl.BlockSpec(memory_space=space)] * len(args),
        scratch_shapes=list(scratch),
        compiler_params=pltpu.CompilerParams(vmem_limit_bytes=mib << 20),
        cost_estimate=pl.CostEstimate(flops=flops, bytes_accessed=moved, transcendentals=0),
        name=name,
    )(*args)


def exchange(x, axes):
    return lax.all_to_all(x, axes, 0, 0, tiled=True)


def on_device(tokens, route_logit, expert_ids, w_gate, w_up, w_down):
    shape = jax.ShapeDtypeStruct
    message = shape((N_EXPERT, MSG, LANES), BF16)
    blocks = shape((N_PART, BLOCK, LANES), BF16)
    sent, aux = call(
        dispatch_kernel, "dispatch", (message, shape((8, TOK), I32)),
        (tokens.T, route_logit.reshape(1, TOK), expert_ids.reshape(1, TOK)),
        space=pltpu.HBM,
        scratch=(
            pltpu.VMEM((WIDTH, TOK), BF16), pltpu.VMEM((1, TOK), F32), pltpu.VMEM((1, TOK), I32),
            pltpu.SemaphoreType.DMA((3,)),
        ),
    )
    arrived = exchange(sent, EXPERT)
    own = call(
        weights_kernel, "weights", shape((MODEL, 3 * FF), BF16), (w_gate, w_up, w_down),
        mib=32, moved=8 << 20, space=pltpu.HBM,
        scratch=(pltpu.VMEM((1, FF, MODEL), BF16), pltpu.SemaphoreType.DMA((4 * N_PART + 1,))),
    )
    other = lax.ppermute(own, "core", [(0, 1), (1, 0)])
    pieces = exchange(call(spread_kernel, "spread", blocks, (arrived,)), TENSOR)
    x_all, hidden = call(
        own_kernel, "own", (shape((ROWS, MODEL), BF16), shape((ROWS, FF), BF16)), (pieces, own),
        flops=50_000_000_000,
    )
    partial = call(
        expert_kernel, "expert", blocks, (x_all, hidden, own, other),
        scratch=(pltpu.VMEM((ROWS, 4 * LANES), F32),), flops=8 * ROWS * MODEL * FF, moved=8 << 20,
    )
    terms = exchange(partial, TENSOR)
    back = call(reduce_kernel, "reduce", message, (terms,))
    returned = exchange(back, EXPERT)
    mixed = call(combine_kernel, "combine", shape((WIDTH, TOK), BF16), (returned, aux))
    return mixed.T


def solution(mesh):
    fine = Mesh(mesh.devices.reshape(16, 2, 2, 4, 2), EXPERT + TENSOR)
    return jax.shard_map(
        on_device,
        mesh=fine,
        in_specs=(
            P(EXPERT, TENSOR),
            P(EXPERT),
            P(EXPERT, None),
            P(EXPERT, None, TENSOR),
            P(EXPERT, None, TENSOR),
            P(EXPERT, TENSOR, None),
        ),
        out_specs=P(EXPERT, TENSOR),
        check_vma=False,
    )
```

```python
import jax
import jax.numpy as jnp
from jax import lax
from jax.experimental import pallas as pl
from jax.experimental.pallas import tpu as pltpu
from jax.sharding import Mesh, PartitionSpec as P

EXPERT = ("z", "yl")
TENSOR = ("yh", "x", "core")
BF16, F32, I32 = jnp.bfloat16, jnp.float32, jnp.int32

N_EXPERT, N_PART, N_CHIP = 32, 16, 8
TOK, WIDTH, FF = 256, 160, 256
MODEL = N_PART * WIDTH
HALF = 5
ROWS = N_EXPERT * HALF
LANES, TAIL = 128, WIDTH - 128
BLOCK = ROWS + N_EXPERT + 8
MSG = 16


def iota(shape, axis):
    return lax.broadcasted_iota(I32, shape, axis)


def slot_rows(ids):
    one_hot = (iota((N_EXPERT, TOK), 0) == ids).astype(F32)
    before = (iota((TOK, TOK), 0) < iota((TOK, TOK), 1)).astype(F32).astype(BF16)
    earlier = jnp.dot(one_hot.astype(BF16), before, preferred_element_type=F32)
    position = jnp.sum(earlier * one_hot, axis=0, keepdims=True).astype(I32)
    second = position >= HALF
    place = jnp.where(second, position - HALF, position)
    base = ids * MSG + jnp.where(second, 8, 0)
    last = place == HALF - 1
    group = jnp.where(last, lax.axis_index("z") // 4, place)
    return base + place, base + jnp.where(last, 6, 5), group


def slot_map(row_main, row_tail):
    at = iota((N_EXPERT * MSG, TOK), 0)
    main = (at == row_main).astype(F32).astype(BF16)
    tail = (at == row_tail).astype(F32).astype(BF16)
    return jnp.concatenate([main, tail], axis=1)


def dispatch_kernel(tok_hbm, logit_hbm, ids_hbm, out_ref, aux_ref, tok_ref, logit_ref, ids_ref, sems):
    copies = [
        pltpu.make_async_copy(src, dst, sems.at[i])
        for i, (src, dst) in enumerate(
            ((ids_hbm, ids_ref), (logit_hbm, logit_ref), (tok_hbm, tok_ref))
        )
    ]
    for copy in copies:
        copy.start()
    copies[0].wait()
    row_main, row_tail, group = slot_rows(ids_ref[...])
    aux_ref[0:1, :] = row_main
    aux_ref[1:2, :] = row_tail
    aux_ref[2:3, :] = group
    aux_ref[3:8, :] = jnp.zeros((5, TOK), I32)
    copies[1].wait()
    copies[2].wait()
    factor = jax.nn.sigmoid(logit_ref[...])
    scaled = (tok_ref[...].astype(F32) * factor).astype(BF16)
    tails = jnp.concatenate([scaled[LANES:, :].astype(F32)] * 4, axis=0)
    tails = jnp.where(iota((LANES, TOK), 0) // TAIL == group, tails, 0.0).astype(BF16)
    both = jnp.concatenate([scaled[:LANES, :], tails], axis=1)
    out = lax.dot_general(
        slot_map(row_main, row_tail), both, (((1,), (1,)), ((), ())), preferred_element_type=F32
    )
    out_ref[...] = out.astype(BF16).reshape(N_EXPERT, MSG, LANES)


def weights_kernel(gate_hbm, up_hbm, down_hbm, out_ref, down_ref, sems):
    down_copy = pltpu.make_async_copy(down_hbm, down_ref, sems.at[4 * N_PART])
    down_copy.start()
    copies = []
    for m in range(N_PART):
        main, tail = LANES * m, N_PART * LANES + TAIL * m
        for size, src, dst in ((LANES, WIDTH * m, main), (TAIL, WIDTH * m + LANES, tail)):
            for i, hbm in enumerate((gate_hbm, up_hbm)):
                target = out_ref.at[i, pl.ds(dst, size)]
                part = hbm.at[0, pl.ds(src, size)]
                copies.append(pltpu.make_async_copy(part, target, sems.at[len(copies)]))
                copies[-1].start()
    down_copy.wait()
    for m in range(N_PART):
        k = m % 4
        at = WIDTH * m - TAIL * k
        window = down_ref[0, :, at : at + LANES]
        if k:
            low = down_ref[0, :, at + LANES : at + 2 * LANES].astype(F32)
            mixed = jnp.where(iota((FF, LANES), 1) >= TAIL * k, window.astype(F32), low)
            window = pltpu.roll(mixed, LANES - TAIL * k, 1).astype(BF16)
        rows, cols = FF * (m // 2), LANES * (m % 2)
        out_ref[2, rows : rows + FF, cols : cols + LANES] = window
    for g in range(4):
        lanes = iota((FF, LANES), 1) // TAIL
        total = jnp.zeros((FF, LANES), F32)
        for k in range(4):
            at = 4 * WIDTH * g + LANES * (k + 1)
            total = jnp.where(lanes == k, down_ref[0, :, at : at + LANES].astype(F32), total)
        rows, cols = FF * (8 + g // 2), LANES * (g % 2)
        out_ref[2, rows : rows + FF, cols : cols + LANES] = total.astype(BF16)
    for copy in copies:
        copy.wait()


def spread_kernel(in_ref, out_ref):
    flat = in_ref[...].reshape(N_EXPERT * MSG, LANES)
    row, col = iota((BLOCK, N_EXPERT * MSG), 0), iota((BLOCK, N_EXPERT * MSG), 1)
    src, q = col // MSG, col % MSG
    for h in range(2):
        want_main = (row == (q - 8 * h) * N_EXPERT + src) & (q >= 8 * h) & (q < 8 * h + HALF)
        want_tail = (row == ROWS + src) & (q == 8 * h + 5)
        want_last = (row == ROWS + N_EXPERT + src % 8) & (q == 8 * h + 6)
        move = (want_main | want_tail | want_last).astype(F32).astype(BF16)
        block = jnp.dot(move, flat, preferred_element_type=F32).astype(BF16)
        for chip in range(N_CHIP):
            out_ref[2 * chip + h] = block


def hidden_units(x, w_ref):
    gate = jnp.dot(x, w_ref[0], preferred_element_type=F32)
    up = jnp.dot(x, w_ref[1], preferred_element_type=F32)
    return (gate / (1.0 + jnp.exp(-gate)) * up).astype(BF16)


def expert_kernel(x_ref, own_hbm, other_hbm, out_ref, own_ref, other_ref, x_all, tails, sems):
    pairs = ((own_hbm, own_ref), (other_hbm, other_ref))
    copies = [
        [pltpu.make_async_copy(src.at[i], dst.at[i], sems.at[side, i]) for i in range(3)]
        for side, (src, dst) in enumerate(pairs)
    ]
    copies[0][0].start()
    copies[0][1].start()
    lanes = iota((N_EXPERT, LANES), 1) // TAIL
    for m in range(N_PART):
        x_all[:, LANES * m : LANES * (m + 1)] = x_ref[m, 0:ROWS, :]
    for g in range(4):
        packed = [x_ref[4 * g + k, ROWS : ROWS + N_EXPERT, :].astype(F32) for k in range(4)]
        ends = [x_ref[4 * g + k, ROWS + N_EXPERT : BLOCK, :].astype(F32) for k in range(4)]
        cols = slice(N_PART * LANES + LANES * g, N_PART * LANES + LANES * (g + 1))
        last = []
        for p in range(4):
            total, end = jnp.zeros((N_EXPERT, LANES), F32), jnp.zeros((8, LANES), F32)
            for k in range(4):
                shift = (TAIL * (k - p)) % LANES
                a = pltpu.roll(packed[k], shift, 1) if shift else packed[k]
                b = pltpu.roll(ends[k], shift, 1) if shift else ends[k]
                total = jnp.where(lanes == k, a, total)
                end = jnp.where(lanes[0:8] == k, b, end)
            x_all[N_EXPERT * p : N_EXPERT * (p + 1), cols] = total.astype(BF16)
            last.append(end)
        x_all[4 * N_EXPERT : ROWS, cols] = jnp.concatenate(last, axis=0).astype(BF16)
    hidden = []
    for side, (_, w_ref) in enumerate(pairs):
        for copy in copies[1][0:2] if side == 0 else (copies[0][2], copies[1][2]):
            copy.start()
        copies[side][0].wait()
        copies[side][1].wait()
        hidden.append(hidden_units(x_all[...], w_ref))
    copies[0][2].wait()
    copies[1][2].wait()
    for i in range(10):
        part = sum(
            jnp.dot(h, w_ref[2, FF * i : FF * (i + 1)], preferred_element_type=F32)
            for h, w_ref in zip(hidden, (own_ref, other_ref))
        )
        if i < 8:
            out_ref[2 * i, 0:ROWS, :] = part[:, 0:LANES].astype(BF16)
            out_ref[2 * i + 1, 0:ROWS, :] = part[:, LANES:].astype(BF16)
        else:
            tails[:, FF * (i - 8) : FF * (i - 7)] = part
    for g in range(4):
        cols = slice(LANES * g, LANES * (g + 1))
        for k in range(4):
            total, end = jnp.zeros((N_EXPERT, LANES), F32), jnp.zeros((8, LANES), F32)
            for p in range(4):
                shift = (TAIL * (p - k)) % LANES
                a = tails[N_EXPERT * p : N_EXPERT * (p + 1), cols]
                b = tails[4 * N_EXPERT + 8 * p : 4 * N_EXPERT + 8 * (p + 1), cols]
                a = pltpu.roll(a, shift, 1) if shift else a
                b = pltpu.roll(b, shift, 1) if shift else b
                total = jnp.where(lanes == p, a, total)
                end = jnp.where(lanes[0:8] == p, b, end)
            rest = jnp.concatenate([total, end], axis=0).astype(BF16)
            out_ref[4 * g + k, ROWS:BLOCK, :] = rest


def reduce_kernel(in_ref, out_ref):
    row, col = iota((N_EXPERT * MSG, BLOCK), 0), iota((N_EXPERT * MSG, BLOCK), 1)
    dst, q = row // MSG, row % MSG
    moved = jnp.zeros((N_EXPERT * MSG, LANES), F32)
    for h in range(2):
        total = in_ref[h].astype(F32)
        for chip in range(1, N_CHIP):
            total = total + in_ref[2 * chip + h].astype(F32)
        want_main = (col == (q - 8 * h) * N_EXPERT + dst) & (q >= 8 * h) & (q < 8 * h + HALF)
        want_tail = (col == ROWS + dst) & (q == 8 * h + 5)
        want_last = (col == ROWS + N_EXPERT + dst % 8) & (q == 8 * h + 6)
        move = (want_main | want_tail | want_last).astype(F32).astype(BF16)
        moved = moved + jnp.dot(move, total.astype(BF16), preferred_element_type=F32)
    out_ref[...] = moved.astype(BF16).reshape(N_EXPERT, MSG, LANES)


def combine_kernel(in_ref, aux_ref, out_ref):
    row_main, row_tail, group = aux_ref[0:1, :], aux_ref[1:2, :], aux_ref[2:3, :]
    flat = in_ref[...].reshape(N_EXPERT * MSG, LANES)
    got = lax.dot_general(
        flat, slot_map(row_main, row_tail), (((0,), (0,)), ((), ())), preferred_element_type=F32
    )
    out_ref[0:LANES, :] = got[:, :TOK].astype(BF16)
    tails = jnp.where(iota((LANES, TOK), 0) // TAIL == group, got[:, TOK:], 0.0)
    tail = tails[0:TAIL] + tails[TAIL : 2 * TAIL] + tails[2 * TAIL : 3 * TAIL] + tails[3 * TAIL :]
    out_ref[LANES:WIDTH, :] = tail.astype(BF16)


def call(kernel, name, out, args, mib=16, scratch=(), flops=0, moved=1 << 20, spaces=pltpu.VMEM):
    spaces = spaces if isinstance(spaces, tuple) else (spaces,) * len(args)
    args = [
        pltpu.with_memory_space_constraint(x, space) if space is pltpu.HBM else x
        for x, space in zip(args, spaces)
    ]
    return pl.pallas_call(
        kernel,
        out_shape=out,
        in_specs=[pl.BlockSpec(memory_space=space) for space in spaces],
        scratch_shapes=list(scratch),
        compiler_params=pltpu.CompilerParams(vmem_limit_bytes=mib << 20),
        cost_estimate=pl.CostEstimate(flops=flops, bytes_accessed=moved, transcendentals=0),
        name=name,
    )(*args)


def exchange(x, axes):
    return lax.all_to_all(x, axes, 0, 0, tiled=True)


def on_device(tokens, route_logit, expert_ids, w_gate, w_up, w_down):
    shape = jax.ShapeDtypeStruct
    message = shape((N_EXPERT, MSG, LANES), BF16)
    blocks = shape((N_PART, BLOCK, LANES), BF16)
    sent, aux = call(
        dispatch_kernel, "dispatch", (message, shape((8, TOK), I32)),
        (tokens.T, route_logit.reshape(1, TOK), expert_ids.reshape(1, TOK)),
        spaces=pltpu.HBM,
        scratch=(
            pltpu.VMEM((WIDTH, TOK), BF16), pltpu.VMEM((1, TOK), F32), pltpu.VMEM((1, TOK), I32),
            pltpu.SemaphoreType.DMA((3,)),
        ),
    )
    arrived = exchange(sent, EXPERT)
    own = call(
        weights_kernel, "weights", shape((3, MODEL, FF), BF16), (w_gate, w_up, w_down),
        mib=32, moved=8 << 20, spaces=pltpu.HBM,
        scratch=(pltpu.VMEM((1, FF, MODEL), BF16), pltpu.SemaphoreType.DMA((4 * N_PART + 1,))),
    )
    other = lax.ppermute(own, "core", [(0, 1), (1, 0)])
    pieces = exchange(call(spread_kernel, "spread", blocks, (arrived,), flops=50_000_000_000), TENSOR)
    partial = call(
        expert_kernel, "expert", blocks, (pieces, own, other), mib=32,
        spaces=(pltpu.VMEM, pltpu.HBM, pltpu.HBM),
        scratch=(pltpu.VMEM((3, MODEL, FF), BF16), pltpu.VMEM((3, MODEL, FF), BF16), pltpu.VMEM((ROWS, MODEL), BF16), pltpu.VMEM((ROWS, 4 * LANES), F32),
                 pltpu.SemaphoreType.DMA((2, 3))),
        flops=12 * ROWS * MODEL * FF, moved=8 << 20,
    )
    terms = exchange(partial, TENSOR)
    back = call(reduce_kernel, "reduce", message, (terms,))
    returned = exchange(back, EXPERT)
    mixed = call(combine_kernel, "combine", shape((WIDTH, TOK), BF16), (returned, aux))
    return mixed.T


def solution(mesh):
    fine = Mesh(mesh.devices.reshape(16, 2, 2, 4, 2), EXPERT + TENSOR)
    return jax.shard_map(
        on_device,
        mesh=fine,
        in_specs=(
            P(EXPERT, TENSOR),
            P(EXPERT),
            P(EXPERT, None),
            P(EXPERT, None, TENSOR),
            P(EXPERT, None, TENSOR),
            P(EXPERT, TENSOR, None),
        ),
        out_specs=P(EXPERT, TENSOR),
        check_vma=False,
    )
```

```python
import jax
import jax.numpy as jnp
from jax import lax
from jax.experimental import pallas as pl
from jax.experimental.pallas import tpu as pltpu
from jax.sharding import Mesh, PartitionSpec as P

EXPERT = ("z", "yl")
TENSOR = ("yh", "x", "core")
PLANE = ("yl",) + TENSOR
BF16, F32, I32 = jnp.bfloat16, jnp.float32, jnp.int32

N_Z, N_YL, N_PART, N_CHIP = 16, 2, 16, 8
N_EXPERT = N_Z * N_YL
TOK, WIDTH, FF = 256, 160, 256
MODEL = N_PART * WIDTH
HALF = 5
PART = N_Z * HALF
ROWS = N_YL * PART
LANES, TAIL = 128, WIDTH - 128
BLOCK = PART + N_Z + 8
MSG = 16


def iota(shape, axis):
    return lax.broadcasted_iota(I32, shape, axis)


def slot_rows(ids):
    one_hot = (iota((N_EXPERT, TOK), 0) == ids).astype(F32)
    before = (iota((TOK, TOK), 0) < iota((TOK, TOK), 1)).astype(F32).astype(BF16)
    earlier = jnp.dot(one_hot.astype(BF16), before, preferred_element_type=F32)
    position = jnp.sum(earlier * one_hot, axis=0, keepdims=True).astype(I32)
    second = position >= HALF
    place = jnp.where(second, position - HALF, position)
    base = ids * MSG + jnp.where(second, 8, 0)
    last = place == HALF - 1
    group = jnp.where(last, lax.axis_index("z") // 8, place)
    return base + place, base + jnp.where(last, 6, 5), group


def slot_map(row_main, row_tail):
    at = iota((N_EXPERT * MSG, TOK), 0)
    main = (at == row_main).astype(F32).astype(BF16)
    tail = (at == row_tail).astype(F32).astype(BF16)
    return jnp.concatenate([main, tail], axis=1)


def dispatch_kernel(tok_hbm, logit_hbm, ids_hbm, out_ref, aux_ref, tok_ref, logit_ref, ids_ref, sems):
    copies = [
        pltpu.make_async_copy(src, dst, sems.at[i])
        for i, (src, dst) in enumerate(
            ((ids_hbm, ids_ref), (logit_hbm, logit_ref), (tok_hbm, tok_ref))
        )
    ]
    for copy in copies:
        copy.start()
    copies[0].wait()
    row_main, row_tail, group = slot_rows(ids_ref[...])
    aux_ref[0:1, :] = row_main
    aux_ref[1:2, :] = row_tail
    aux_ref[2:3, :] = group
    aux_ref[3:8, :] = jnp.zeros((5, TOK), I32)
    copies[1].wait()
    copies[2].wait()
    factor = jax.nn.sigmoid(logit_ref[...])
    scaled = (tok_ref[...].astype(F32) * factor).astype(BF16)
    tails = jnp.concatenate([scaled[LANES:, :].astype(F32)] * 4, axis=0)
    tails = jnp.where(iota((LANES, TOK), 0) // TAIL == group, tails, 0.0).astype(BF16)
    both = jnp.concatenate([scaled[:LANES, :], tails], axis=1)
    out = lax.dot_general(
        slot_map(row_main, row_tail), both, (((1,), (1,)), ((), ())), preferred_element_type=F32
    )
    out_ref[...] = out.astype(BF16).reshape(N_Z, N_YL * MSG, LANES)


def weights_kernel(gate_hbm, up_hbm, down_hbm, out_ref, down_ref, sems):
    down_copy = pltpu.make_async_copy(down_hbm, down_ref, sems.at[4 * N_PART])
    down_copy.start()
    copies = []
    for m in range(N_PART):
        main, tail = LANES * m, N_PART * LANES + TAIL * m
        for size, src, dst in ((LANES, WIDTH * m, main), (TAIL, WIDTH * m + LANES, tail)):
            for i, hbm in enumerate((gate_hbm, up_hbm)):
                target = out_ref.at[i, pl.ds(dst, size)]
                part = hbm.at[0, pl.ds(src, size)]
                copies.append(pltpu.make_async_copy(part, target, sems.at[len(copies)]))
                copies[-1].start()
    down_copy.wait()
    for m in range(N_PART):
        k = m % 4
        at = WIDTH * m - TAIL * k
        window = down_ref[0, :, at : at + LANES]
        if k:
            low = down_ref[0, :, at + LANES : at + 2 * LANES].astype(F32)
            mixed = jnp.where(iota((FF, LANES), 1) >= TAIL * k, window.astype(F32), low)
            window = pltpu.roll(mixed, LANES - TAIL * k, 1).astype(BF16)
        rows, cols = FF * (m // 2), LANES * (m % 2)
        out_ref[2, rows : rows + FF, cols : cols + LANES] = window
    for g in range(4):
        lanes = iota((FF, LANES), 1) // TAIL
        total = jnp.zeros((FF, LANES), F32)
        for k in range(4):
            at = 4 * WIDTH * g + LANES * (k + 1)
            total = jnp.where(lanes == k, down_ref[0, :, at : at + LANES].astype(F32), total)
        rows, cols = FF * (8 + g // 2), LANES * (g % 2)
        out_ref[2, rows : rows + FF, cols : cols + LANES] = total.astype(BF16)
    for copy in copies:
        copy.wait()


def packed_row(slot):
    src, q = slot // 8, slot % 8
    row = jnp.where(q < HALF, q * N_Z + src, PART + src)
    row = jnp.where(q == 6, PART + N_Z + src % 8, row)
    return jnp.where(q == 7, -1, row)


def spread_kernel(in_ref, out_ref):
    move = iota((BLOCK, 8 * N_Z), 0) == packed_row(iota((1, 8 * N_Z), 1))
    move = move.astype(F32).astype(BF16)
    for yl in range(N_YL):
        for h in range(2):
            at = MSG * yl + 8 * h
            rows = in_ref[:, at : at + 8, :].astype(F32).reshape(8 * N_Z, LANES).astype(BF16)
            block = jnp.dot(move, rows, preferred_element_type=F32).astype(BF16)
            for chip in range(N_CHIP):
                out_ref[N_PART * yl + 2 * chip + h] = block


def hidden_units(x, w_ref):
    gate = jnp.dot(x, w_ref[0], preferred_element_type=F32)
    up = jnp.dot(x, w_ref[1], preferred_element_type=F32)
    return (gate / (1.0 + jnp.exp(-gate)) * up).astype(BF16)


def expert_kernel(x_ref, own_hbm, other_hbm, out_ref, own_ref, other_ref, x_all, total, sems):
    copies = {}
    for side, (src, dst) in enumerate(((own_hbm, own_ref), (other_hbm, other_ref))):
        for i in range(2):
            copies[side, i] = pltpu.make_async_copy(src.at[i], dst.at[i], sems.at[side, i])
        for n, rows in enumerate((slice(8 * FF, MODEL), slice(0, 4 * FF), slice(4 * FF, 8 * FF))):
            part, target = src.at[2, rows], dst.at[2, rows]
            copies[side, 2 + n] = pltpu.make_async_copy(part, target, sems.at[side, 2 + n])
    for i in range(5):
        copies[0, i].start()
    lanes = iota((N_Z, LANES), 1) // TAIL

    def turn(x, groups):
        shift = (TAIL * groups) % LANES
        return pltpu.roll(x, shift, 1) if shift else x

    def pick(parts):
        whole = jnp.zeros(parts[0].shape, F32)
        for k, part in enumerate(parts):
            whole = jnp.where(lanes[0 : part.shape[0]] == k, part, whole)
        return whole

    for yl in range(N_YL):
        for m in range(N_PART):
            x_all[PART * yl : PART * (yl + 1), LANES * m : LANES * (m + 1)] = x_ref[
                N_PART * yl + m, 0:PART, :
            ]
        for g in range(4):
            parts = [N_PART * yl + 4 * g + k for k in range(4)]
            packed = [x_ref[i, PART : PART + N_Z, :].astype(F32) for i in parts]
            ends = [x_ref[i, PART + N_Z : BLOCK, :].astype(F32) for i in parts]
            cols = slice(N_PART * LANES + LANES * g, N_PART * LANES + LANES * (g + 1))
            made = [pick([turn(packed[k], k - p) for k in range(4)]) for p in range(4)]
            made += [pick([turn(ends[k], k - j) for k in range(4)]) for j in range(2)]
            x_all[PART * yl : PART * (yl + 1), cols] = jnp.concatenate(made, axis=0).astype(BF16)

    def wait(side, *which):
        for i in which:
            copies[side, i].wait()

    def down(hidden, w_ref, i):
        return jnp.dot(hidden, w_ref[2, FF * i : FF * (i + 1)], preferred_element_type=F32)

    for i in range(5):
        copies[1, i].start()
    wait(0, 0, 1)
    hidden = hidden_units(x_all[...], own_ref)
    wait(0, 2, 3, 4)
    for i in range(10):
        total[:, FF * i : FF * (i + 1)] = down(hidden, own_ref, i)
    wait(1, 0, 1)
    hidden = hidden_units(x_all[...], other_ref)
    wait(1, 2)
    for i in (8, 9):
        total[:, FF * i : FF * (i + 1)] += down(hidden, other_ref, i)
    for yl in range(N_YL):
        for g in range(4):
            cols = slice(N_PART * LANES + LANES * g, N_PART * LANES + LANES * (g + 1))
            main = [total[PART * yl + N_Z * p : PART * yl + N_Z * (p + 1), cols] for p in range(4)]
            first = PART * yl + 4 * N_Z
            ends = [total[first + 8 * j : first + 8 * (j + 1), cols] for j in range(2)]
            for k in range(4):
                made = [pick([turn(main[p], p - k) for p in range(4)])]
                made.append(pick([turn(ends[j], j - k) for j in range(2)]))
                rest = jnp.concatenate(made, axis=0).astype(BF16)
                out_ref[N_PART * yl + 4 * g + k, PART:BLOCK, :] = rest
    for i in range(8):
        if i % 4 == 0:
            wait(1, 3 + i // 4)
        part = (total[:, FF * i : FF * (i + 1)] + down(hidden, other_ref, i)).astype(BF16)
        for yl in range(N_YL):
            rows = slice(PART * yl, PART * (yl + 1))
            out_ref[N_PART * yl + 2 * i, 0:PART, :] = part[rows, 0:LANES]
            out_ref[N_PART * yl + 2 * i + 1, 0:PART, :] = part[rows, LANES:]


def reduce_kernel(in_ref, out_ref):
    move = iota((8 * N_Z, BLOCK), 1) == packed_row(iota((8 * N_Z, 1), 0))
    move = move.astype(F32).astype(BF16)
    for yl in range(N_YL):
        for h in range(2):
            total = in_ref[N_PART * yl + h].astype(F32)
            for chip in range(1, N_CHIP):
                total = total + in_ref[N_PART * yl + 2 * chip + h].astype(F32)
            rows = jnp.dot(move, total.astype(BF16), preferred_element_type=F32)
            at = MSG * yl + 8 * h
            out_ref[:, at : at + 8, :] = rows.reshape(N_Z, 8, LANES).astype(BF16)


def combine_kernel(in_ref, aux_ref, out_ref):
    row_main, row_tail, group = aux_ref[0:1, :], aux_ref[1:2, :], aux_ref[2:3, :]
    flat = in_ref[...].reshape(N_EXPERT * MSG, LANES)
    got = lax.dot_general(
        flat, slot_map(row_main, row_tail), (((0,), (0,)), ((), ())), preferred_element_type=F32
    )
    out_ref[0:LANES, :] = got[:, :TOK].astype(BF16)
    tails = jnp.where(iota((LANES, TOK), 0) // TAIL == group, got[:, TOK:], 0.0)
    tail = tails[0:TAIL] + tails[TAIL : 2 * TAIL] + tails[2 * TAIL : 3 * TAIL] + tails[3 * TAIL :]
    out_ref[LANES:WIDTH, :] = tail.astype(BF16)


def call(kernel, name, out, args, mib=16, scratch=(), flops=0, moved=1 << 20, spaces=pltpu.VMEM):
    spaces = spaces if isinstance(spaces, tuple) else (spaces,) * len(args)
    args = [
        pltpu.with_memory_space_constraint(x, space) if space is pltpu.HBM else x
        for x, space in zip(args, spaces)
    ]
    return pl.pallas_call(
        kernel,
        out_shape=out,
        in_specs=[pl.BlockSpec(memory_space=space) for space in spaces],
        scratch_shapes=list(scratch),
        compiler_params=pltpu.CompilerParams(vmem_limit_bytes=mib << 20),
        cost_estimate=pl.CostEstimate(flops=flops, bytes_accessed=moved, transcendentals=0),
        name=name,
    )(*args)


def exchange(x, axes):
    return lax.all_to_all(x, axes, 0, 0, tiled=True)


def on_device(tokens, route_logit, expert_ids, w_gate, w_up, w_down):
    shape = jax.ShapeDtypeStruct
    message = shape((N_Z, N_YL * MSG, LANES), BF16)
    blocks = shape((N_YL * N_PART, BLOCK, LANES), BF16)
    sent, aux = call(
        dispatch_kernel, "dispatch", (message, shape((8, TOK), I32)),
        (tokens.T, route_logit.reshape(1, TOK), expert_ids.reshape(1, TOK)),
        spaces=pltpu.HBM,
        scratch=(
            pltpu.VMEM((WIDTH, TOK), BF16), pltpu.VMEM((1, TOK), F32), pltpu.VMEM((1, TOK), I32),
            pltpu.SemaphoreType.DMA((3,)),
        ),
    )
    arrived = exchange(sent, "z")
    own = call(
        weights_kernel, "weights", shape((3, MODEL, FF), BF16), (w_gate, w_up, w_down),
        mib=32, moved=8 << 20, spaces=pltpu.HBM,
        scratch=(pltpu.VMEM((1, FF, MODEL), BF16), pltpu.SemaphoreType.DMA((4 * N_PART + 1,))),
    )
    other = lax.ppermute(own, "core", [(0, 1), (1, 0)])
    pieces = exchange(call(spread_kernel, "spread", blocks, (arrived,), flops=50_000_000_000), PLANE)
    partial = call(
        expert_kernel, "expert", blocks, (pieces, own, other), mib=32,
        spaces=(pltpu.VMEM, pltpu.HBM, pltpu.HBM),
        scratch=(pltpu.VMEM((3, MODEL, FF), BF16), pltpu.VMEM((3, MODEL, FF), BF16), pltpu.VMEM((ROWS, MODEL), BF16), pltpu.VMEM((ROWS, MODEL), F32),
                 pltpu.SemaphoreType.DMA((2, 5))),
        flops=12 * ROWS * MODEL * FF, moved=8 << 20,
    )
    terms = exchange(partial, PLANE)
    back = call(reduce_kernel, "reduce", message, (terms,))
    returned = exchange(back, "z")
    mixed = call(combine_kernel, "combine", shape((WIDTH, TOK), BF16), (returned, aux))
    return mixed.T


def solution(mesh):
    fine = Mesh(mesh.devices.reshape(16, 2, 2, 4, 2), EXPERT + TENSOR)
    return jax.shard_map(
        on_device,
        mesh=fine,
        in_specs=(
            P(EXPERT, TENSOR),
            P(EXPERT),
            P(EXPERT, None),
            P(EXPERT, None, TENSOR),
            P(EXPERT, None, TENSOR),
            P(EXPERT, TENSOR, None),
        ),
        out_specs=P(EXPERT, TENSOR),
        check_vma=False,
    )
```

```python
import jax
import jax.numpy as jnp
from jax import lax
from jax.experimental import pallas as pl
from jax.experimental.pallas import tpu as pltpu
from jax.sharding import Mesh, PartitionSpec as P

EXPERT = ("z", "yl")
TENSOR = ("yh", "x", "core")
PLANE = ("yl",) + TENSOR
BF16, F32, I32 = jnp.bfloat16, jnp.float32, jnp.int32

N_Z, N_YL, N_PART, N_CHIP = 16, 2, 16, 8
N_EXPERT = N_Z * N_YL
TOK, WIDTH, FF = 256, 160, 256
MODEL = N_PART * WIDTH
HALF = 5
PART = N_Z * HALF
ROWS = N_YL * PART
LANES, TAIL = 128, WIDTH - 128
BLOCK = PART + N_Z + 8
MSG = 16


def iota(shape, axis):
    return lax.broadcasted_iota(I32, shape, axis)


def slot_rows(ids):
    one_hot = (iota((N_EXPERT, TOK), 0) == ids).astype(F32)
    before = (iota((TOK, TOK), 0) < iota((TOK, TOK), 1)).astype(F32).astype(BF16)
    earlier = jnp.dot(one_hot.astype(BF16), before, preferred_element_type=F32)
    position = jnp.sum(earlier * one_hot, axis=0, keepdims=True).astype(I32)
    second = position >= HALF
    place = jnp.where(second, position - HALF, position)
    base = ids * MSG + jnp.where(second, 8, 0)
    last = place == HALF - 1
    group = jnp.where(last, lax.axis_index("z") // 8, place)
    return base + place, base + jnp.where(last, 6, 5), group


def slot_map(row_main, row_tail):
    at = iota((N_EXPERT * MSG, TOK), 0)
    main = (at == row_main).astype(F32).astype(BF16)
    tail = (at == row_tail).astype(F32).astype(BF16)
    return jnp.concatenate([main, tail], axis=1)


def dispatch_kernel(
    tok_hbm, logit_hbm, ids_hbm, gate_hbm, up_hbm, down_hbm, out_ref, aux_ref, own_ref,
    tok_ref, logit_ref, ids_ref, down_ref, sems,
):
    first = ((ids_hbm, ids_ref), (logit_hbm, logit_ref), (tok_hbm, tok_ref), (down_hbm, down_ref))
    loads = [pltpu.make_async_copy(src, dst, sems.at[i]) for i, (src, dst) in enumerate(first)]
    for load in loads:
        load.start()
    copies = [
        pltpu.make_async_copy(hbm.at[0], own_ref.at[i], sems.at[4 + i])
        for i, hbm in enumerate((gate_hbm, up_hbm))
    ]
    for copy in copies:
        copy.start()
    loads[0].wait()
    row_main, row_tail, group = slot_rows(ids_ref[...])
    aux_ref[0:1, :] = row_main
    aux_ref[1:2, :] = row_tail
    aux_ref[2:3, :] = group
    aux_ref[3:8, :] = jnp.zeros((5, TOK), I32)
    moves = slot_map(row_main, row_tail)
    loads[1].wait()
    loads[2].wait()
    factor = jax.nn.sigmoid(logit_ref[...])
    scaled = (tok_ref[...].astype(F32) * factor).astype(BF16)
    tails = jnp.concatenate([scaled[LANES:, :].astype(F32)] * 4, axis=0)
    tails = jnp.where(iota((LANES, TOK), 0) // TAIL == group, tails, 0.0).astype(BF16)
    both = jnp.concatenate([scaled[:LANES, :], tails], axis=1)
    out = lax.dot_general(moves, both, (((1,), (1,)), ((), ())), preferred_element_type=F32)
    out_ref[...] = out.astype(BF16).reshape(N_Z, N_YL * MSG, LANES)

    loads[3].wait()
    for m in range(N_PART):
        k = m % 4
        at = WIDTH * m - TAIL * k
        window = down_ref[0, :, at : at + LANES]
        if k:
            low = down_ref[0, :, at + LANES : at + 2 * LANES].astype(F32)
            mixed = jnp.where(iota((FF, LANES), 1) >= TAIL * k, window.astype(F32), low)
            window = pltpu.roll(mixed, LANES - TAIL * k, 1).astype(BF16)
        rows, cols = FF * (m // 2), LANES * (m % 2)
        own_ref[2, rows : rows + FF, cols : cols + LANES] = window
    lanes = iota((FF, LANES), 1) // TAIL
    for g in range(4):
        total = jnp.zeros((FF, LANES), F32)
        for k in range(4):
            at = 4 * WIDTH * g + LANES * (k + 1)
            total = jnp.where(lanes == k, down_ref[0, :, at : at + LANES].astype(F32), total)
        rows, cols = FF * (8 + g // 2), LANES * (g % 2)
        own_ref[2, rows : rows + FF, cols : cols + LANES] = total.astype(BF16)
    for copy in copies:
        copy.wait()


def packed_row(slot):
    src, q = slot // 8, slot % 8
    row = jnp.where(q < HALF, q * N_Z + src, PART + src)
    row = jnp.where(q == 6, PART + N_Z + src % 8, row)
    return jnp.where(q == 7, -1, row)


def spread_kernel(in_ref, out_ref):
    move = iota((BLOCK, 8 * N_Z), 0) == packed_row(iota((1, 8 * N_Z), 1))
    move = move.astype(F32).astype(BF16)
    for yl in range(N_YL):
        for h in range(2):
            at = MSG * yl + 8 * h
            rows = in_ref[:, at : at + 8, :].astype(F32).reshape(8 * N_Z, LANES).astype(BF16)
            block = jnp.dot(move, rows, preferred_element_type=F32).astype(BF16)
            for chip in range(N_CHIP):
                out_ref[N_PART * yl + 2 * chip + h] = block


def hidden_units(x_ref, w_ref):
    halves = []
    for i in range(2):
        total = jnp.zeros((ROWS, FF), F32)
        for n in range(MODEL // FF):
            if n < 8:
                starts, size = [WIDTH * m for m in (2 * n, 2 * n + 1)], LANES
            else:
                starts, size = [WIDTH * m + LANES for m in range(8 * n - 64, 8 * n - 56)], TAIL
            rows = jnp.concatenate([w_ref[i, at : at + size] for at in starts], axis=0)
            x = x_ref[:, FF * n : FF * (n + 1)]
            total = total + jnp.dot(x, rows, preferred_element_type=F32)
        halves.append(total)
    gate, up = halves
    return (gate / (1.0 + jnp.exp(-gate)) * up).astype(BF16)


def expert_kernel(x_ref, own_ref, other_ref, out_ref, x_all, total):
    lanes = iota((N_Z, LANES), 1) // TAIL

    def turn(x, groups):
        shift = (TAIL * groups) % LANES
        return pltpu.roll(x, shift, 1) if shift else x

    def pick(parts):
        whole = jnp.zeros(parts[0].shape, F32)
        for k, part in enumerate(parts):
            whole = jnp.where(lanes[0 : part.shape[0]] == k, part, whole)
        return whole

    for yl in range(N_YL):
        for m in range(N_PART):
            x_all[PART * yl : PART * (yl + 1), LANES * m : LANES * (m + 1)] = x_ref[
                N_PART * yl + m, 0:PART, :
            ]
        for g in range(4):
            parts = [N_PART * yl + 4 * g + k for k in range(4)]
            packed = [x_ref[i, PART : PART + N_Z, :].astype(F32) for i in parts]
            ends = [x_ref[i, PART + N_Z : BLOCK, :].astype(F32) for i in parts]
            cols = slice(N_PART * LANES + LANES * g, N_PART * LANES + LANES * (g + 1))
            made = [pick([turn(packed[k], k - p) for k in range(4)]) for p in range(4)]
            made += [pick([turn(ends[k], k - j) for k in range(4)]) for j in range(2)]
            x_all[PART * yl : PART * (yl + 1), cols] = jnp.concatenate(made, axis=0).astype(BF16)

    def down(hidden, w_ref, i):
        return jnp.dot(hidden, w_ref[2, FF * i : FF * (i + 1)], preferred_element_type=F32)

    own = hidden_units(x_all, own_ref)
    other = hidden_units(x_all, other_ref)

    def chunk(i):
        return down(own, own_ref, i) + down(other, other_ref, i)

    for i in (8, 9):
        total[:, FF * (i - 8) : FF * (i - 7)] = chunk(i)
    for yl in range(N_YL):
        for g in range(4):
            cols = slice(LANES * g, LANES * (g + 1))
            main = [total[PART * yl + N_Z * p : PART * yl + N_Z * (p + 1), cols] for p in range(4)]
            first = PART * yl + 4 * N_Z
            ends = [total[first + 8 * j : first + 8 * (j + 1), cols] for j in range(2)]
            for k in range(4):
                made = [pick([turn(main[p], p - k) for p in range(4)])]
                made.append(pick([turn(ends[j], j - k) for j in range(2)]))
                rest = jnp.concatenate(made, axis=0).astype(BF16)
                out_ref[N_PART * yl + 4 * g + k, PART:BLOCK, :] = rest
    for i in range(8):
        part = chunk(i).astype(BF16)
        for yl in range(N_YL):
            rows = slice(PART * yl, PART * (yl + 1))
            out_ref[N_PART * yl + 2 * i, 0:PART, :] = part[rows, 0:LANES]
            out_ref[N_PART * yl + 2 * i + 1, 0:PART, :] = part[rows, LANES:]


def reduce_kernel(in_ref, out_ref):
    move = iota((8 * N_Z, BLOCK), 1) == packed_row(iota((8 * N_Z, 1), 0))
    move = move.astype(F32).astype(BF16)
    for yl in range(N_YL):
        for h in range(2):
            total = in_ref[N_PART * yl + h].astype(F32)
            for chip in range(1, N_CHIP):
                total = total + in_ref[N_PART * yl + 2 * chip + h].astype(F32)
            rows = jnp.dot(move, total.astype(BF16), preferred_element_type=F32)
            at = MSG * yl + 8 * h
            out_ref[:, at : at + 8, :] = rows.reshape(N_Z, 8, LANES).astype(BF16)


def combine_kernel(in_ref, aux_ref, out_ref):
    row_main, row_tail, group = aux_ref[0:1, :], aux_ref[1:2, :], aux_ref[2:3, :]
    flat = in_ref[...].reshape(N_EXPERT * MSG, LANES)
    got = lax.dot_general(
        flat, slot_map(row_main, row_tail), (((0,), (0,)), ((), ())), preferred_element_type=F32
    )
    out_ref[0:LANES, :] = got[:, :TOK].astype(BF16)
    tails = jnp.where(iota((LANES, TOK), 0) // TAIL == group, got[:, TOK:], 0.0)
    tail = tails[0:TAIL] + tails[TAIL : 2 * TAIL] + tails[2 * TAIL : 3 * TAIL] + tails[3 * TAIL :]
    out_ref[LANES:WIDTH, :] = tail.astype(BF16)


def call(kernel, name, out, args, mib=16, scratch=(), flops=0, moved=1 << 20, spaces=pltpu.VMEM):
    spaces = spaces if isinstance(spaces, tuple) else (spaces,) * len(args)
    args = [
        pltpu.with_memory_space_constraint(x, space) if space is pltpu.HBM else x
        for x, space in zip(args, spaces)
    ]
    return pl.pallas_call(
        kernel,
        out_shape=out,
        in_specs=[pl.BlockSpec(memory_space=space) for space in spaces],
        scratch_shapes=list(scratch),
        compiler_params=pltpu.CompilerParams(vmem_limit_bytes=mib << 20),
        cost_estimate=pl.CostEstimate(flops=flops, bytes_accessed=moved, transcendentals=0),
        name=name,
    )(*args)


def exchange(x, axes):
    return lax.all_to_all(x, axes, 0, 0, tiled=True)


def on_device(tokens, route_logit, expert_ids, w_gate, w_up, w_down):
    shape = jax.ShapeDtypeStruct
    message = shape((N_Z, N_YL * MSG, LANES), BF16)
    blocks = shape((N_YL * N_PART, BLOCK, LANES), BF16)
    weights = shape((3, MODEL, FF), BF16)
    sent, aux, own = call(
        dispatch_kernel, "dispatch", (message, shape((8, TOK), I32), weights),
        (
            tokens.T, route_logit.reshape(1, TOK), expert_ids.reshape(1, TOK),
            w_gate, w_up, w_down,
        ),
        spaces=pltpu.HBM, moved=8 << 20,
        scratch=(
            pltpu.VMEM((WIDTH, TOK), BF16), pltpu.VMEM((1, TOK), F32), pltpu.VMEM((1, TOK), I32),
            pltpu.VMEM((1, FF, MODEL), BF16),
            pltpu.SemaphoreType.DMA((6,)),
        ),
    )
    other = lax.ppermute(own, "core", [(0, 1), (1, 0)])
    arrived = exchange(sent, "z")
    pieces = exchange(call(spread_kernel, "spread", blocks, (arrived,)), PLANE)
    partial = call(
        expert_kernel, "expert", blocks, (pieces, own, other), mib=32,
        scratch=(pltpu.VMEM((ROWS, MODEL), BF16), pltpu.VMEM((ROWS, 4 * LANES), F32)),
        flops=12 * ROWS * MODEL * FF, moved=8 << 20,
    )
    terms = exchange(partial, PLANE)
    back = call(reduce_kernel, "reduce", message, (terms,))
    returned = exchange(back, "z")
    mixed = call(combine_kernel, "combine", shape((WIDTH, TOK), BF16), (returned, aux))
    return mixed.T


def solution(mesh):
    fine = Mesh(mesh.devices.reshape(16, 2, 2, 4, 2), EXPERT + TENSOR)
    return jax.shard_map(
        on_device,
        mesh=fine,
        in_specs=(
            P(EXPERT, TENSOR),
            P(EXPERT),
            P(EXPERT, None),
            P(EXPERT, None, TENSOR),
            P(EXPERT, None, TENSOR),
            P(EXPERT, TENSOR, None),
        ),
        out_specs=P(EXPERT, TENSOR),
        check_vma=False,
    )
```

```python
import jax
import jax.numpy as jnp
from jax import lax
from jax.experimental import pallas as pl
from jax.experimental.pallas import tpu as pltpu
from jax.sharding import Mesh, PartitionSpec as P

EXPERT = ("z", "yl")
TENSOR = ("yh", "x", "core")
PLANE = ("yl",) + TENSOR
BF16, F32, I32 = jnp.bfloat16, jnp.float32, jnp.int32

N_Z, N_YL, N_PART, N_CHIP = 16, 2, 16, 8
N_EXPERT = N_Z * N_YL
TOK, WIDTH, FF = 256, 160, 256
MODEL = N_PART * WIDTH
HALF = 5
PART = N_Z * HALF
ROWS = N_YL * PART
LANES, TAIL = 128, WIDTH - 128
BLOCK = PART + N_Z + 8
MSG = 16


def iota(shape, axis):
    return lax.broadcasted_iota(I32, shape, axis)


def slot_rows(ids):
    one_hot = (iota((N_EXPERT, TOK), 0) == ids).astype(F32)
    before = (iota((TOK, TOK), 0) < iota((TOK, TOK), 1)).astype(F32).astype(BF16)
    earlier = jnp.dot(one_hot.astype(BF16), before, preferred_element_type=F32)
    position = jnp.sum(earlier * one_hot, axis=0, keepdims=True).astype(I32)
    second = position >= HALF
    place = jnp.where(second, position - HALF, position)
    base = ids * MSG + jnp.where(second, 8, 0)
    last = place == HALF - 1
    group = jnp.where(last, lax.axis_index("z") // 8, place)
    return base + place, base + jnp.where(last, 6, 5), group


def slot_map(row_main, row_tail):
    at = iota((N_EXPERT * MSG, TOK), 0)
    main = (at == row_main).astype(F32).astype(BF16)
    tail = (at == row_tail).astype(F32).astype(BF16)
    return jnp.concatenate([main, tail], axis=1)


def dispatch_kernel(tok_hbm, logit_hbm, ids_hbm, out_ref, aux_ref, tok_ref, logit_ref, ids_ref, sems):
    copies = [
        pltpu.make_async_copy(src, dst, sems.at[i])
        for i, (src, dst) in enumerate(
            ((ids_hbm, ids_ref), (logit_hbm, logit_ref), (tok_hbm, tok_ref))
        )
    ]
    for copy in copies:
        copy.start()
    copies[0].wait()
    row_main, row_tail, group = slot_rows(ids_ref[...])
    aux_ref[0:1, :] = row_main
    aux_ref[1:2, :] = row_tail
    aux_ref[2:3, :] = group
    aux_ref[3:8, :] = jnp.zeros((5, TOK), I32)
    copies[1].wait()
    copies[2].wait()
    factor = jax.nn.sigmoid(logit_ref[...])
    scaled = (tok_ref[...].astype(F32) * factor).astype(BF16)
    tails = jnp.concatenate([scaled[LANES:, :].astype(F32)] * 4, axis=0)
    tails = jnp.where(iota((LANES, TOK), 0) // TAIL == group, tails, 0.0).astype(BF16)
    both = jnp.concatenate([scaled[:LANES, :], tails], axis=1)
    out = lax.dot_general(
        slot_map(row_main, row_tail), both, (((1,), (1,)), ((), ())), preferred_element_type=F32
    )
    out_ref[...] = out.astype(BF16).reshape(N_Z, N_YL * MSG, LANES)


def packed_row(slot):
    src, q = slot // 8, slot % 8
    row = jnp.where(q < HALF, q * N_Z + src, PART + src)
    row = jnp.where(q == 6, PART + N_Z + src % 8, row)
    return jnp.where(q == 7, -1, row)


def spread_kernel(in_ref, out_ref):
    move = iota((BLOCK, 8 * N_Z), 0) == packed_row(iota((1, 8 * N_Z), 1))
    move = move.astype(F32).astype(BF16)
    for yl in range(N_YL):
        for h in range(2):
            at = MSG * yl + 8 * h
            rows = in_ref[:, at : at + 8, :].astype(F32).reshape(8 * N_Z, LANES).astype(BF16)
            block = jnp.dot(move, rows, preferred_element_type=F32).astype(BF16)
            for chip in range(N_CHIP):
                out_ref[N_PART * yl + 2 * chip + h] = block


def hidden_units(x_ref, weights):
    halves = []
    for w_ref in weights:
        total = jnp.zeros((ROWS, FF), F32)
        for n in range(MODEL // FF):
            if n < 8:
                starts, size = [WIDTH * m for m in (2 * n, 2 * n + 1)], LANES
            else:
                starts, size = [WIDTH * m + LANES for m in range(8 * n - 64, 8 * n - 56)], TAIL
            rows = jnp.concatenate([w_ref[0, at : at + size, :] for at in starts], axis=0)
            x = x_ref[:, FF * n : FF * (n + 1)]
            total = total + jnp.dot(x, rows, preferred_element_type=F32)
        halves.append(total)
    gate, up = halves
    return (gate / (1.0 + jnp.exp(-gate)) * up).astype(BF16)


def expert_kernel(x_ref, *refs):
    own_refs, other_refs, (out_ref, down_ref, x_all, total, sem) = refs[0:3], refs[3:6], refs[6:]
    load = pltpu.make_async_copy(other_refs[2], down_ref, sem)
    load.start()
    lanes = iota((N_Z, LANES), 1) // TAIL

    def turn(x, groups):
        shift = (TAIL * groups) % LANES
        return pltpu.roll(x, shift, 1) if shift else x

    def pick(parts):
        whole = jnp.zeros(parts[0].shape, F32)
        for k, part in enumerate(parts):
            whole = jnp.where(lanes[0 : part.shape[0]] == k, part, whole)
        return whole

    for yl in range(N_YL):
        for m in range(N_PART):
            x_all[PART * yl : PART * (yl + 1), LANES * m : LANES * (m + 1)] = x_ref[
                N_PART * yl + m, 0:PART, :
            ]
        for g in range(4):
            parts = [N_PART * yl + 4 * g + k for k in range(4)]
            packed = [x_ref[i, PART : PART + N_Z, :].astype(F32) for i in parts]
            ends = [x_ref[i, PART + N_Z : BLOCK, :].astype(F32) for i in parts]
            cols = slice(N_PART * LANES + LANES * g, N_PART * LANES + LANES * (g + 1))
            made = [pick([turn(packed[k], k - p) for k in range(4)]) for p in range(4)]
            made += [pick([turn(ends[k], k - j) for k in range(4)]) for j in range(2)]
            x_all[PART * yl : PART * (yl + 1), cols] = jnp.concatenate(made, axis=0).astype(BF16)

    hidden = hidden_units(x_all, own_refs[0:2])
    for n in range(MODEL // FF):
        cols = slice(FF * n, FF * (n + 1))
        total[:, cols] = jnp.dot(hidden, own_refs[2][0, :, cols], preferred_element_type=F32)
    hidden = hidden_units(x_all, other_refs[0:2])
    load.wait()
    for n in range(MODEL // FF):
        cols = slice(FF * n, FF * (n + 1))
        total[:, cols] += jnp.dot(hidden, down_ref[0, :, cols], preferred_element_type=F32)
    whole = iota((PART, LANES), 1) // TAIL
    for yl in range(N_YL):
        rows = slice(PART * yl, PART * (yl + 1))
        for g in range(4):
            tails = jnp.zeros((PART, LANES), F32)
            for k in range(4):
                at = 4 * WIDTH * g + LANES * k
                main, after = total[rows, at : at + LANES], total[rows, at + LANES : at + 2 * LANES]
                tails = jnp.where(whole == k, after, tails)
                main = turn(jnp.where(whole >= k, main, after), -k)
                out_ref[N_PART * yl + 4 * g + k, 0:PART, :] = main.astype(BF16)
            main = [tails[N_Z * p : N_Z * (p + 1)] for p in range(4)]
            ends = [tails[4 * N_Z + 8 * j : 4 * N_Z + 8 * (j + 1)] for j in range(2)]
            for k in range(4):
                made = [pick([turn(main[p], p - k) for p in range(4)])]
                made.append(pick([turn(ends[j], j - k) for j in range(2)]))
                rest = jnp.concatenate(made, axis=0).astype(BF16)
                out_ref[N_PART * yl + 4 * g + k, PART:BLOCK, :] = rest


def reduce_kernel(in_ref, out_ref):
    move = iota((8 * N_Z, BLOCK), 1) == packed_row(iota((8 * N_Z, 1), 0))
    move = move.astype(F32).astype(BF16)
    for yl in range(N_YL):
        for h in range(2):
            total = in_ref[N_PART * yl + h].astype(F32)
            for chip in range(1, N_CHIP):
                total = total + in_ref[N_PART * yl + 2 * chip + h].astype(F32)
            rows = jnp.dot(move, total.astype(BF16), preferred_element_type=F32)
            at = MSG * yl + 8 * h
            out_ref[:, at : at + 8, :] = rows.reshape(N_Z, 8, LANES).astype(BF16)


def combine_kernel(in_ref, aux_ref, out_ref):
    row_main, row_tail, group = aux_ref[0:1, :], aux_ref[1:2, :], aux_ref[2:3, :]
    flat = in_ref[...].reshape(N_EXPERT * MSG, LANES)
    got = lax.dot_general(
        flat, slot_map(row_main, row_tail), (((0,), (0,)), ((), ())), preferred_element_type=F32
    )
    out_ref[0:LANES, :] = got[:, :TOK].astype(BF16)
    tails = jnp.where(iota((LANES, TOK), 0) // TAIL == group, got[:, TOK:], 0.0)
    tail = tails[0:TAIL] + tails[TAIL : 2 * TAIL] + tails[2 * TAIL : 3 * TAIL] + tails[3 * TAIL :]
    out_ref[LANES:WIDTH, :] = tail.astype(BF16)


def call(kernel, name, out, args, mib=16, scratch=(), flops=0, moved=1 << 20, spaces=pltpu.VMEM):
    spaces = spaces if isinstance(spaces, tuple) else (spaces,) * len(args)
    args = [
        pltpu.with_memory_space_constraint(x, space) if space is pltpu.HBM else x
        for x, space in zip(args, spaces)
    ]
    return pl.pallas_call(
        kernel,
        out_shape=out,
        in_specs=[pl.BlockSpec(memory_space=space) for space in spaces],
        scratch_shapes=list(scratch),
        compiler_params=pltpu.CompilerParams(vmem_limit_bytes=mib << 20),
        cost_estimate=pl.CostEstimate(flops=flops, bytes_accessed=moved, transcendentals=0),
        name=name,
    )(*args)


def exchange(x, axes):
    return lax.all_to_all(x, axes, 0, 0, tiled=True)


def on_device(tokens, route_logit, expert_ids, w_gate, w_up, w_down):
    shape = jax.ShapeDtypeStruct
    message = shape((N_Z, N_YL * MSG, LANES), BF16)
    blocks = shape((N_YL * N_PART, BLOCK, LANES), BF16)
    sent, aux = call(
        dispatch_kernel, "dispatch", (message, shape((8, TOK), I32)),
        (tokens.T, route_logit.reshape(1, TOK), expert_ids.reshape(1, TOK)),
        spaces=pltpu.HBM,
        scratch=(
            pltpu.VMEM((WIDTH, TOK), BF16), pltpu.VMEM((1, TOK), F32), pltpu.VMEM((1, TOK), I32),
            pltpu.SemaphoreType.DMA((3,)),
        ),
    )
    arrived = exchange(sent, "z")
    own = (w_gate, w_up, w_down)
    other = [lax.ppermute(w, "core", [(0, 1), (1, 0)]) for w in own]
    packed = call(spread_kernel, "spread", blocks, (arrived,), flops=50_000_000_000)
    packed, *other = lax.optimization_barrier((packed, *other))
    pieces = exchange(packed, PLANE)
    partial = call(
        expert_kernel, "expert", blocks, (pieces, *own, *other), mib=20,
        spaces=(pltpu.VMEM,) * 6 + (pltpu.HBM,),
        scratch=(
            pltpu.VMEM((1, FF, MODEL), BF16), pltpu.VMEM((ROWS, MODEL), BF16),
            pltpu.VMEM((ROWS, MODEL), F32), pltpu.SemaphoreType.DMA,
        ),
        flops=12 * ROWS * MODEL * FF, moved=8 << 20,
    )
    terms = exchange(partial, PLANE)
    back = call(reduce_kernel, "reduce", message, (terms,))
    returned = exchange(back, "z")
    mixed = call(combine_kernel, "combine", shape((WIDTH, TOK), BF16), (returned, aux))
    return mixed.T


def solution(mesh):
    fine = Mesh(mesh.devices.reshape(16, 2, 2, 4, 2), EXPERT + TENSOR)
    return jax.shard_map(
        on_device,
        mesh=fine,
        in_specs=(
            P(EXPERT, TENSOR),
            P(EXPERT),
            P(EXPERT, None),
            P(EXPERT, None, TENSOR),
            P(EXPERT, None, TENSOR),
            P(EXPERT, TENSOR, None),
        ),
        out_specs=P(EXPERT, TENSOR),
        check_vma=False,
    )
```

```python
import jax
import jax.numpy as jnp
from jax import lax
from jax.experimental import pallas as pl
from jax.experimental.pallas import tpu as pltpu
from jax.sharding import Mesh, PartitionSpec as P

EXPERT = ("z", "yl")
TENSOR = ("yh", "x", "core")
PLANE = ("yl",) + TENSOR
BF16, F32, I32 = jnp.bfloat16, jnp.float32, jnp.int32

N_Z, N_YL, N_PART, N_CHIP = 16, 2, 16, 8
N_EXPERT = N_Z * N_YL
TOK, WIDTH, FF = 256, 160, 256
MODEL = N_PART * WIDTH
HALF = 5
PART = N_Z * HALF
ROWS = N_YL * PART
LANES, TAIL = 128, WIDTH - 128
BLOCK = PART + N_Z + 8
MSG = 16


def iota(shape, axis):
    return lax.broadcasted_iota(I32, shape, axis)


def slot_rows(ids):
    one_hot = (iota((N_EXPERT, TOK), 0) == ids).astype(F32)
    before = (iota((TOK, TOK), 0) < iota((TOK, TOK), 1)).astype(F32).astype(BF16)
    earlier = jnp.dot(one_hot.astype(BF16), before, preferred_element_type=F32)
    position = jnp.sum(earlier * one_hot, axis=0, keepdims=True).astype(I32)
    second = position >= HALF
    place = jnp.where(second, position - HALF, position)
    base = ids * MSG + jnp.where(second, 8, 0)
    last = place == HALF - 1
    group = jnp.where(last, lax.axis_index("z") // 8, place)
    return base + place, base + jnp.where(last, 6, 5), group


def slot_map(row_main, row_tail):
    at = iota((N_EXPERT * MSG, TOK), 0)
    main = (at == row_main).astype(F32).astype(BF16)
    tail = (at == row_tail).astype(F32).astype(BF16)
    return jnp.concatenate([main, tail], axis=1)


def dispatch_kernel(tok_hbm, logit_hbm, ids_hbm, out_ref, aux_ref, tok_ref, logit_ref, ids_ref, sems):
    copies = [
        pltpu.make_async_copy(src, dst, sems.at[i])
        for i, (src, dst) in enumerate(
            ((ids_hbm, ids_ref), (logit_hbm, logit_ref), (tok_hbm, tok_ref))
        )
    ]
    for copy in copies:
        copy.start()
    copies[0].wait()
    row_main, row_tail, group = slot_rows(ids_ref[...])
    aux_ref[0:1, :] = row_main
    aux_ref[1:2, :] = row_tail
    aux_ref[2:3, :] = group
    aux_ref[3:8, :] = jnp.zeros((5, TOK), I32)
    copies[1].wait()
    copies[2].wait()
    factor = jax.nn.sigmoid(logit_ref[...])
    scaled = (tok_ref[...].astype(F32) * factor).astype(BF16)
    tails = jnp.concatenate([scaled[LANES:, :].astype(F32)] * 4, axis=0)
    tails = jnp.where(iota((LANES, TOK), 0) // TAIL == group, tails, 0.0).astype(BF16)
    both = jnp.concatenate([scaled[:LANES, :], tails], axis=1)
    out = lax.dot_general(
        slot_map(row_main, row_tail), both, (((1,), (1,)), ((), ())), preferred_element_type=F32
    )
    out_ref[...] = out.astype(BF16).reshape(N_Z, N_YL * MSG, LANES)


def weights_kernel(gate_hbm, up_hbm, down_hbm, out_ref, down_ref, sems):
    down_copy = pltpu.make_async_copy(down_hbm, down_ref, sems.at[2])
    down_copy.start()
    copies = [
        pltpu.make_async_copy(hbm.at[0], out_ref.at[i], sems.at[i])
        for i, hbm in enumerate((gate_hbm, up_hbm))
    ]
    for copy in copies:
        copy.start()
    down_copy.wait()
    for m in range(N_PART):
        k = m % 4
        at = WIDTH * m - TAIL * k
        window = down_ref[0, :, at : at + LANES]
        if k:
            low = down_ref[0, :, at + LANES : at + 2 * LANES].astype(F32)
            mixed = jnp.where(iota((FF, LANES), 1) >= TAIL * k, window.astype(F32), low)
            window = pltpu.roll(mixed, LANES - TAIL * k, 1).astype(BF16)
        rows, cols = FF * (m // 2), LANES * (m % 2)
        out_ref[2, rows : rows + FF, cols : cols + LANES] = window
    for g in range(4):
        lanes = iota((FF, LANES), 1) // TAIL
        total = jnp.zeros((FF, LANES), F32)
        for k in range(4):
            at = 4 * WIDTH * g + LANES * (k + 1)
            total = jnp.where(lanes == k, down_ref[0, :, at : at + LANES].astype(F32), total)
        rows, cols = FF * (8 + g // 2), LANES * (g % 2)
        out_ref[2, rows : rows + FF, cols : cols + LANES] = total.astype(BF16)
    for copy in copies:
        copy.wait()


def packed_row(slot):
    src, q = slot // 8, slot % 8
    row = jnp.where(q < HALF, q * N_Z + src, PART + src)
    row = jnp.where(q == 6, PART + N_Z + src % 8, row)
    return jnp.where(q == 7, -1, row)


def spread_kernel(in_ref, out_ref):
    move = iota((BLOCK, 8 * N_Z), 0) == packed_row(iota((1, 8 * N_Z), 1))
    move = move.astype(F32).astype(BF16)
    for yl in range(N_YL):
        for h in range(2):
            at = MSG * yl + 8 * h
            rows = in_ref[:, at : at + 8, :].astype(F32).reshape(8 * N_Z, LANES).astype(BF16)
            block = jnp.dot(move, rows, preferred_element_type=F32).astype(BF16)
            for chip in range(N_CHIP):
                out_ref[N_PART * yl + 2 * chip + h] = block


def hidden_units(x_ref, weights):
    halves = []
    for w_ref in weights:
        total = jnp.zeros((ROWS, FF), F32)
        for n in range(MODEL // FF):
            if n < 8:
                starts, size = [WIDTH * m for m in (2 * n, 2 * n + 1)], LANES
            else:
                starts, size = [WIDTH * m + LANES for m in range(8 * n - 64, 8 * n - 56)], TAIL
            rows = jnp.concatenate([w_ref[at : at + size, :] for at in starts], axis=0)
            x = x_ref[:, FF * n : FF * (n + 1)]
            total = total + jnp.dot(x, rows, preferred_element_type=F32)
        halves.append(total)
    gate, up = halves
    return (gate / (1.0 + jnp.exp(-gate)) * up).astype(BF16)


def expert_kernel(
    x_ref, gate_ref, up_ref, own_hbm, other_hbm, out_ref, other_ref, down_ref, x_all, total, sems
):
    copies = [pltpu.make_async_copy(other_hbm.at[i], other_ref.at[i], sems.at[i]) for i in range(3)]
    copies.append(pltpu.make_async_copy(own_hbm.at[2], down_ref, sems.at[3]))
    for i in (0, 1):
        copies[i].start()
    lanes = iota((N_Z, LANES), 1) // TAIL

    def turn(x, groups):
        shift = (TAIL * groups) % LANES
        return pltpu.roll(x, shift, 1) if shift else x

    def pick(parts):
        whole = jnp.zeros(parts[0].shape, F32)
        for k, part in enumerate(parts):
            whole = jnp.where(lanes[0 : part.shape[0]] == k, part, whole)
        return whole

    for yl in range(N_YL):
        for m in range(N_PART):
            x_all[PART * yl : PART * (yl + 1), LANES * m : LANES * (m + 1)] = x_ref[
                N_PART * yl + m, 0:PART, :
            ]
        for g in range(4):
            parts = [N_PART * yl + 4 * g + k for k in range(4)]
            packed = [x_ref[i, PART : PART + N_Z, :].astype(F32) for i in parts]
            ends = [x_ref[i, PART + N_Z : BLOCK, :].astype(F32) for i in parts]
            cols = slice(N_PART * LANES + LANES * g, N_PART * LANES + LANES * (g + 1))
            made = [pick([turn(packed[k], k - p) for k in range(4)]) for p in range(4)]
            made += [pick([turn(ends[k], k - j) for k in range(4)]) for j in range(2)]
            x_all[PART * yl : PART * (yl + 1), cols] = jnp.concatenate(made, axis=0).astype(BF16)

    for i in (3, 2):
        copies[i].start()
    own = hidden_units(x_all, (gate_ref.at[0], up_ref.at[0]))
    copies[0].wait()
    copies[1].wait()
    other = hidden_units(x_all, (other_ref.at[0], other_ref.at[1]))
    copies[3].wait()
    copies[2].wait()

    def chunk(i):
        rows = slice(FF * i, FF * (i + 1))
        part = jnp.dot(other, other_ref[2, rows], preferred_element_type=F32)
        return jnp.dot(own, down_ref[rows], preferred_element_type=F32) + part

    for i in (8, 9):
        total[:, FF * i : FF * (i + 1)] = chunk(i)
    for yl in range(N_YL):
        for g in range(4):
            cols = slice(N_PART * LANES + LANES * g, N_PART * LANES + LANES * (g + 1))
            main = [total[PART * yl + N_Z * p : PART * yl + N_Z * (p + 1), cols] for p in range(4)]
            first = PART * yl + 4 * N_Z
            ends = [total[first + 8 * j : first + 8 * (j + 1), cols] for j in range(2)]
            for k in range(4):
                made = [pick([turn(main[p], p - k) for p in range(4)])]
                made.append(pick([turn(ends[j], j - k) for j in range(2)]))
                rest = jnp.concatenate(made, axis=0).astype(BF16)
                out_ref[N_PART * yl + 4 * g + k, PART:BLOCK, :] = rest
    for i in range(8):
        part = chunk(i).astype(BF16)
        for yl in range(N_YL):
            rows = slice(PART * yl, PART * (yl + 1))
            out_ref[N_PART * yl + 2 * i, 0:PART, :] = part[rows, 0:LANES]
            out_ref[N_PART * yl + 2 * i + 1, 0:PART, :] = part[rows, LANES:]


def reduce_kernel(in_ref, out_ref):
    move = iota((8 * N_Z, BLOCK), 1) == packed_row(iota((8 * N_Z, 1), 0))
    move = move.astype(F32).astype(BF16)
    for yl in range(N_YL):
        for h in range(2):
            total = in_ref[N_PART * yl + h].astype(F32)
            for chip in range(1, N_CHIP):
                total = total + in_ref[N_PART * yl + 2 * chip + h].astype(F32)
            rows = jnp.dot(move, total.astype(BF16), preferred_element_type=F32)
            at = MSG * yl + 8 * h
            out_ref[:, at : at + 8, :] = rows.reshape(N_Z, 8, LANES).astype(BF16)


def combine_kernel(in_ref, aux_ref, out_ref):
    row_main, row_tail, group = aux_ref[0:1, :], aux_ref[1:2, :], aux_ref[2:3, :]
    flat = in_ref[...].reshape(N_EXPERT * MSG, LANES)
    got = lax.dot_general(
        flat, slot_map(row_main, row_tail), (((0,), (0,)), ((), ())), preferred_element_type=F32
    )
    out_ref[0:LANES, :] = got[:, :TOK].astype(BF16)
    tails = jnp.where(iota((LANES, TOK), 0) // TAIL == group, got[:, TOK:], 0.0)
    tail = tails[0:TAIL] + tails[TAIL : 2 * TAIL] + tails[2 * TAIL : 3 * TAIL] + tails[3 * TAIL :]
    out_ref[LANES:WIDTH, :] = tail.astype(BF16)


def call(kernel, name, out, args, mib=16, scratch=(), flops=0, moved=1 << 20, spaces=pltpu.VMEM):
    spaces = spaces if isinstance(spaces, tuple) else (spaces,) * len(args)
    args = [
        pltpu.with_memory_space_constraint(x, space) if space is pltpu.HBM else x
        for x, space in zip(args, spaces)
    ]
    return pl.pallas_call(
        kernel,
        out_shape=out,
        in_specs=[pl.BlockSpec(memory_space=space) for space in spaces],
        scratch_shapes=list(scratch),
        compiler_params=pltpu.CompilerParams(vmem_limit_bytes=mib << 20),
        cost_estimate=pl.CostEstimate(flops=flops, bytes_accessed=moved, transcendentals=0),
        name=name,
    )(*args)


def exchange(x, axes):
    return lax.all_to_all(x, axes, 0, 0, tiled=True)


def on_device(tokens, route_logit, expert_ids, w_gate, w_up, w_down):
    shape = jax.ShapeDtypeStruct
    message = shape((N_Z, N_YL * MSG, LANES), BF16)
    blocks = shape((N_YL * N_PART, BLOCK, LANES), BF16)
    sent, aux = call(
        dispatch_kernel, "dispatch", (message, shape((8, TOK), I32)),
        (tokens.T, route_logit.reshape(1, TOK), expert_ids.reshape(1, TOK)),
        spaces=pltpu.HBM,
        scratch=(
            pltpu.VMEM((WIDTH, TOK), BF16), pltpu.VMEM((1, TOK), F32), pltpu.VMEM((1, TOK), I32),
            pltpu.SemaphoreType.DMA((3,)),
        ),
    )
    arrived = exchange(sent, "z")
    own = call(
        weights_kernel, "weights", shape((3, MODEL, FF), BF16), (w_gate, w_up, w_down),
        mib=32, moved=8 << 20, spaces=pltpu.HBM,
        scratch=(pltpu.VMEM((1, FF, MODEL), BF16), pltpu.SemaphoreType.DMA((3,))),
    )
    other = lax.ppermute(own, "core", [(0, 1), (1, 0)])
    pieces = exchange(call(spread_kernel, "spread", blocks, (arrived,), flops=50_000_000_000), PLANE)
    partial = call(
        expert_kernel, "expert", blocks, (pieces, w_gate, w_up, own, other), mib=20,
        spaces=(pltpu.VMEM,) * 3 + (pltpu.HBM,) * 2,
        scratch=(
            pltpu.VMEM((3, MODEL, FF), BF16), pltpu.VMEM((MODEL, FF), BF16),
            pltpu.VMEM((ROWS, MODEL), BF16), pltpu.VMEM((ROWS, MODEL), F32),
            pltpu.SemaphoreType.DMA((4,)),
        ),
        flops=12 * ROWS * MODEL * FF, moved=8 << 20,
    )
    terms = exchange(partial, PLANE)
    back = call(reduce_kernel, "reduce", message, (terms,))
    returned = exchange(back, "z")
    mixed = call(combine_kernel, "combine", shape((WIDTH, TOK), BF16), (returned, aux))
    return mixed.T


def solution(mesh):
    fine = Mesh(mesh.devices.reshape(16, 2, 2, 4, 2), EXPERT + TENSOR)
    return jax.shard_map(
        on_device,
        mesh=fine,
        in_specs=(
            P(EXPERT, TENSOR),
            P(EXPERT),
            P(EXPERT, None),
            P(EXPERT, None, TENSOR),
            P(EXPERT, None, TENSOR),
            P(EXPERT, TENSOR, None),
        ),
        out_specs=P(EXPERT, TENSOR),
        check_vma=False,
    )
```

```python
import jax
import jax.numpy as jnp
from jax import lax
from jax.experimental import pallas as pl
from jax.experimental.pallas import tpu as pltpu
from jax.sharding import Mesh, PartitionSpec as P

EXPERT = ("z", "yl")
TENSOR = ("yh", "x", "core")
PLANE = ("yl",) + TENSOR
BF16, F32, I32 = jnp.bfloat16, jnp.float32, jnp.int32

N_Z, N_YL, N_PART, N_CHIP = 16, 2, 16, 8
N_EXPERT = N_Z * N_YL
TOK, WIDTH, FF = 256, 160, 256
MODEL = N_PART * WIDTH
HALF = 5
PART = N_Z * HALF
ROWS = N_YL * PART
LANES, TAIL = 128, WIDTH - 128
BLOCK = PART + N_Z + 8
PAIRS = 13
FLAT = PAIRS * N_Z * 2


def iota(shape, axis):
    return lax.broadcasted_iota(I32, shape, axis)


def flat_row(row, z):
    return row // 2 * (2 * N_Z) + 2 * z + row % 2


def load_messages(ref):
    parts = [ref[:, :, LANES * v : LANES * (v + 1)] for v in range(PAIRS)]
    return jnp.concatenate([p.reshape(2 * N_Z, LANES) for p in parts], axis=0)


def store_messages(ref, rows):
    for v in range(PAIRS):
        part = rows[2 * N_Z * v : 2 * N_Z * (v + 1)].reshape(N_Z, 2, LANES)
        ref[:, :, LANES * v : LANES * (v + 1)] = part.astype(BF16)


def slot_rows(ids):
    one_hot = (iota((N_EXPERT, TOK), 0) == ids).astype(F32)
    before = (iota((TOK, TOK), 0) < iota((TOK, TOK), 1)).astype(F32).astype(BF16)
    earlier = jnp.dot(one_hot.astype(BF16), before, preferred_element_type=F32)
    position = jnp.sum(earlier * one_hot, axis=0, keepdims=True).astype(I32)
    second = position >= HALF
    place = jnp.where(second, position - HALF, position)
    upper = jnp.where(second, 1, 0)
    to_z, yl = ids // N_YL, ids % N_YL
    first = 6 * (2 * yl + upper)
    last = place == HALF - 1
    group = jnp.where(last, 2 * upper + lax.axis_index("z") // 8, place)
    tail = jnp.where(last, 24 + yl, first + 5)
    return flat_row(first + place, to_z), flat_row(tail, to_z), group


def slot_map(row_main, row_tail):
    at = iota((FLAT, TOK), 0)
    main = (at == row_main).astype(F32).astype(BF16)
    tail = (at == row_tail).astype(F32).astype(BF16)
    return jnp.concatenate([main, tail], axis=1)


def dispatch_kernel(tok_hbm, logit_hbm, ids_hbm, out_ref, aux_ref, tok_ref, logit_ref, ids_ref, sems):
    copies = [
        pltpu.make_async_copy(src, dst, sems.at[i])
        for i, (src, dst) in enumerate(
            ((ids_hbm, ids_ref), (logit_hbm, logit_ref), (tok_hbm, tok_ref))
        )
    ]
    for copy in copies:
        copy.start()
    copies[0].wait()
    row_main, row_tail, group = slot_rows(ids_ref[...])
    aux_ref[0:1, :] = row_main
    aux_ref[1:2, :] = row_tail
    aux_ref[2:3, :] = group
    aux_ref[3:8, :] = jnp.zeros((5, TOK), I32)
    copies[1].wait()
    copies[2].wait()
    factor = jax.nn.sigmoid(logit_ref[...])
    scaled = (tok_ref[...].astype(F32) * factor).astype(BF16)
    tails = jnp.concatenate([scaled[LANES:, :].astype(F32)] * 4, axis=0)
    tails = jnp.where(iota((LANES, TOK), 0) // TAIL == group, tails, 0.0).astype(BF16)
    both = jnp.concatenate([scaled[:LANES, :], tails], axis=1)
    out = lax.dot_general(
        slot_map(row_main, row_tail), both, (((1,), (1,)), ((), ())), preferred_element_type=F32
    )
    store_messages(out_ref, out)


def weights_kernel(gate_hbm, up_hbm, down_hbm, out_ref, down_ref, sems):
    down_copy = pltpu.make_async_copy(down_hbm, down_ref, sems.at[2])
    down_copy.start()
    copies = [
        pltpu.make_async_copy(hbm.at[0], out_ref.at[i], sems.at[i])
        for i, hbm in enumerate((gate_hbm, up_hbm))
    ]
    for copy in copies:
        copy.start()
    down_copy.wait()
    for m in range(N_PART):
        k = m % 4
        at = WIDTH * m - TAIL * k
        window = down_ref[0, :, at : at + LANES]
        if k:
            low = down_ref[0, :, at + LANES : at + 2 * LANES].astype(F32)
            mixed = jnp.where(iota((FF, LANES), 1) >= TAIL * k, window.astype(F32), low)
            window = pltpu.roll(mixed, LANES - TAIL * k, 1).astype(BF16)
        rows, cols = FF * (m // 2), LANES * (m % 2)
        out_ref[2, rows : rows + FF, cols : cols + LANES] = window
    for g in range(4):
        lanes = iota((FF, LANES), 1) // TAIL
        total = jnp.zeros((FF, LANES), F32)
        for k in range(4):
            at = 4 * WIDTH * g + LANES * (k + 1)
            total = jnp.where(lanes == k, down_ref[0, :, at : at + LANES].astype(F32), total)
        rows, cols = FF * (8 + g // 2), LANES * (g % 2)
        out_ref[2, rows : rows + FF, cols : cols + LANES] = total.astype(BF16)
    for copy in copies:
        copy.wait()


MAIN = 6 * N_Z


def main_row(flat):
    return (flat // (2 * N_Z) * 2 + flat % 2) * N_Z + flat % (2 * N_Z) // 2


def last_row(flat):
    return flat % 2 * 8 + flat // 2 % 8


def select(rows, cols):
    return (rows == cols).astype(F32).astype(BF16)


def spread_kernel(in_ref, out_ref):
    flat = load_messages(in_ref)
    move = select(iota((MAIN, MAIN), 0), main_row(iota((1, MAIN), 1)))
    last = select(iota((16, 2 * N_Z), 0), last_row(iota((1, 2 * N_Z), 1)))
    ends = jnp.dot(last, flat[2 * N_YL * MAIN :], preferred_element_type=F32)
    for part in range(2 * N_YL):
        yl, h = part // 2, part % 2
        rows = flat[MAIN * part : MAIN * (part + 1)]
        block = jnp.dot(move, rows, preferred_element_type=F32)
        end = ends[8 * yl : 8 * (yl + 1)]
        if h:
            end = pltpu.roll(end, LANES // 2, 1)
        block = jnp.concatenate([block, end], axis=0).astype(BF16)
        for chip in range(N_CHIP):
            out_ref[N_PART * yl + 2 * chip + h] = block


def hidden_units(x_ref, weights):
    halves = []
    for w_ref in weights:
        total = jnp.zeros((ROWS, FF), F32)
        for n in range(MODEL // FF):
            if n < 8:
                starts, size = [WIDTH * m for m in (2 * n, 2 * n + 1)], LANES
            else:
                starts, size = [WIDTH * m + LANES for m in range(8 * n - 64, 8 * n - 56)], TAIL
            rows = jnp.concatenate([w_ref[at : at + size, :] for at in starts], axis=0)
            x = x_ref[:, FF * n : FF * (n + 1)]
            total = total + jnp.dot(x, rows, preferred_element_type=F32)
        halves.append(total)
    gate, up = halves
    return (gate / (1.0 + jnp.exp(-gate)) * up).astype(BF16)


def expert_kernel(
    x_ref, gate_ref, up_ref, own_hbm, other_hbm, out_ref, other_ref, down_ref, x_all, total, sems
):
    copies = [pltpu.make_async_copy(other_hbm.at[i], other_ref.at[i], sems.at[i]) for i in range(3)]
    copies.append(pltpu.make_async_copy(own_hbm.at[2], down_ref, sems.at[3]))
    for i in (0, 1):
        copies[i].start()
    lanes = iota((N_Z, LANES), 1) // TAIL

    def turn(x, groups):
        shift = (TAIL * groups) % LANES
        return pltpu.roll(x, shift, 1) if shift else x

    def pick(parts):
        whole = jnp.zeros(parts[0].shape, F32)
        for k, part in enumerate(parts):
            whole = jnp.where(lanes[0 : part.shape[0]] == k, part, whole)
        return whole

    for yl in range(N_YL):
        for m in range(N_PART):
            x_all[PART * yl : PART * (yl + 1), LANES * m : LANES * (m + 1)] = x_ref[
                N_PART * yl + m, 0:PART, :
            ]
        for g in range(4):
            parts = [N_PART * yl + 4 * g + k for k in range(4)]
            packed = [x_ref[i, PART : PART + N_Z, :].astype(F32) for i in parts]
            ends = [x_ref[i, PART + N_Z : BLOCK, :].astype(F32) for i in parts]
            cols = slice(N_PART * LANES + LANES * g, N_PART * LANES + LANES * (g + 1))
            made = [pick([turn(packed[k], k - p) for k in range(4)]) for p in range(4)]
            made += [pick([turn(ends[k], k - j) for k in range(4)]) for j in range(2)]
            x_all[PART * yl : PART * (yl + 1), cols] = jnp.concatenate(made, axis=0).astype(BF16)

    for i in (3, 2):
        copies[i].start()
    own = hidden_units(x_all, (gate_ref.at[0], up_ref.at[0]))
    copies[0].wait()
    copies[1].wait()
    other = hidden_units(x_all, (other_ref.at[0], other_ref.at[1]))
    copies[3].wait()
    copies[2].wait()

    def chunk(i):
        rows = slice(FF * i, FF * (i + 1))
        part = jnp.dot(other, other_ref[2, rows], preferred_element_type=F32)
        return jnp.dot(own, down_ref[rows], preferred_element_type=F32) + part

    for i in (8, 9):
        total[:, FF * i : FF * (i + 1)] = chunk(i)
    for yl in range(N_YL):
        for g in range(4):
            cols = slice(N_PART * LANES + LANES * g, N_PART * LANES + LANES * (g + 1))
            main = [total[PART * yl + N_Z * p : PART * yl + N_Z * (p + 1), cols] for p in range(4)]
            first = PART * yl + 4 * N_Z
            ends = [total[first + 8 * j : first + 8 * (j + 1), cols] for j in range(2)]
            for k in range(4):
                made = [pick([turn(main[p], p - k) for p in range(4)])]
                made.append(pick([turn(ends[j], j - k) for j in range(2)]))
                rest = jnp.concatenate(made, axis=0).astype(BF16)
                out_ref[N_PART * yl + 4 * g + k, PART:BLOCK, :] = rest
    for i in range(8):
        part = chunk(i).astype(BF16)
        for yl in range(N_YL):
            rows = slice(PART * yl, PART * (yl + 1))
            out_ref[N_PART * yl + 2 * i, 0:PART, :] = part[rows, 0:LANES]
            out_ref[N_PART * yl + 2 * i + 1, 0:PART, :] = part[rows, LANES:]


def reduce_kernel(in_ref, out_ref):
    move = select(iota((MAIN, MAIN), 1), main_row(iota((MAIN, 1), 0)))
    last = select(iota((2 * N_Z, 16), 1), last_row(iota((2 * N_Z, 1), 0)))
    moved, ends = [], []
    for part in range(2 * N_YL):
        yl, h = part // 2, part % 2
        total = in_ref[N_PART * yl + h].astype(F32)
        for chip in range(1, N_CHIP):
            total = total + in_ref[N_PART * yl + 2 * chip + h].astype(F32)
        rows = total[:MAIN].astype(BF16)
        moved.append(jnp.dot(move, rows, preferred_element_type=F32))
        if h:
            ends[yl] = ends[yl] + pltpu.roll(total[MAIN:], LANES // 2, 1)
        else:
            ends.append(total[MAIN:])
    ends = jnp.concatenate(ends, axis=0).astype(BF16)
    moved.append(jnp.dot(last, ends, preferred_element_type=F32))
    store_messages(out_ref, jnp.concatenate(moved, axis=0))


def combine_kernel(in_ref, aux_ref, out_ref):
    row_main, row_tail, group = aux_ref[0:1, :], aux_ref[1:2, :], aux_ref[2:3, :]
    flat = load_messages(in_ref)
    got = lax.dot_general(
        flat, slot_map(row_main, row_tail), (((0,), (0,)), ((), ())), preferred_element_type=F32
    )
    out_ref[0:LANES, :] = got[:, :TOK].astype(BF16)
    tails = jnp.where(iota((LANES, TOK), 0) // TAIL == group, got[:, TOK:], 0.0)
    tail = tails[0:TAIL] + tails[TAIL : 2 * TAIL] + tails[2 * TAIL : 3 * TAIL] + tails[3 * TAIL :]
    out_ref[LANES:WIDTH, :] = tail.astype(BF16)


def call(kernel, name, out, args, mib=16, scratch=(), flops=0, moved=1 << 20, spaces=pltpu.VMEM):
    spaces = spaces if isinstance(spaces, tuple) else (spaces,) * len(args)
    args = [
        pltpu.with_memory_space_constraint(x, space) if space is pltpu.HBM else x
        for x, space in zip(args, spaces)
    ]
    return pl.pallas_call(
        kernel,
        out_shape=out,
        in_specs=[pl.BlockSpec(memory_space=space) for space in spaces],
        scratch_shapes=list(scratch),
        compiler_params=pltpu.CompilerParams(vmem_limit_bytes=mib << 20),
        cost_estimate=pl.CostEstimate(flops=flops, bytes_accessed=moved, transcendentals=0),
        name=name,
    )(*args)


def exchange(x, axes):
    return lax.all_to_all(x, axes, 0, 0, tiled=True)


def on_device(tokens, route_logit, expert_ids, w_gate, w_up, w_down):
    shape = jax.ShapeDtypeStruct
    message = shape((N_Z, 2, PAIRS * LANES), BF16)
    blocks = shape((N_YL * N_PART, BLOCK, LANES), BF16)
    sent, aux = call(
        dispatch_kernel, "dispatch", (message, shape((8, TOK), I32)),
        (tokens.T, route_logit.reshape(1, TOK), expert_ids.reshape(1, TOK)),
        spaces=pltpu.HBM,
        scratch=(
            pltpu.VMEM((WIDTH, TOK), BF16), pltpu.VMEM((1, TOK), F32), pltpu.VMEM((1, TOK), I32),
            pltpu.SemaphoreType.DMA((3,)),
        ),
    )
    arrived = exchange(sent, "z")
    own = call(
        weights_kernel, "weights", shape((3, MODEL, FF), BF16), (w_gate, w_up, w_down),
        mib=32, moved=8 << 20, spaces=pltpu.HBM,
        scratch=(pltpu.VMEM((1, FF, MODEL), BF16), pltpu.SemaphoreType.DMA((3,))),
    )
    other = lax.ppermute(own, "core", [(0, 1), (1, 0)])
    pieces = exchange(call(spread_kernel, "spread", blocks, (arrived,), flops=50_000_000_000), PLANE)
    partial = call(
        expert_kernel, "expert", blocks, (pieces, w_gate, w_up, own, other), mib=20,
        spaces=(pltpu.VMEM,) * 3 + (pltpu.HBM,) * 2,
        scratch=(
            pltpu.VMEM((3, MODEL, FF), BF16), pltpu.VMEM((MODEL, FF), BF16),
            pltpu.VMEM((ROWS, MODEL), BF16), pltpu.VMEM((ROWS, MODEL), F32),
            pltpu.SemaphoreType.DMA((4,)),
        ),
        flops=12 * ROWS * MODEL * FF, moved=8 << 20,
    )
    terms = exchange(partial, PLANE)
    back = call(reduce_kernel, "reduce", message, (terms,))
    returned = exchange(back, "z")
    mixed = call(combine_kernel, "combine", shape((WIDTH, TOK), BF16), (returned, aux))
    return mixed.T


def solution(mesh):
    fine = Mesh(mesh.devices.reshape(16, 2, 2, 4, 2), EXPERT + TENSOR)
    return jax.shard_map(
        on_device,
        mesh=fine,
        in_specs=(
            P(EXPERT, TENSOR),
            P(EXPERT),
            P(EXPERT, None),
            P(EXPERT, None, TENSOR),
            P(EXPERT, None, TENSOR),
            P(EXPERT, TENSOR, None),
        ),
        out_specs=P(EXPERT, TENSOR),
        check_vma=False,
    )
```

```python
import jax
import jax.numpy as jnp
from jax import lax
from jax.experimental import pallas as pl
from jax.experimental.pallas import tpu as pltpu
from jax.sharding import Mesh, PartitionSpec as P

EXPERT = ("z", "yl")
TENSOR = ("yh", "x", "core")
PLANE = ("yh", "yl", "x", "core")
BF16, F32, I32 = jnp.bfloat16, jnp.float32, jnp.int32

N_Z, N_YL, N_PART, N_CHIP = 16, 2, 16, 8
N_EXPERT = N_Z * N_YL
TOK, WIDTH, FF = 256, 160, 256
MODEL = N_PART * WIDTH
HALF = 5
PART = N_Z * HALF
ROWS = N_YL * PART
LANES, TAIL = 128, WIDTH - 128
BLOCK = PART + N_Z + 8
PAIRS = 13
FLAT = PAIRS * N_Z * 2


def place(yl, part):
    return part // 8 * 16 + 8 * yl + part % 8


def iota(shape, axis):
    return lax.broadcasted_iota(I32, shape, axis)


def flat_row(row, z):
    return row // 2 * (2 * N_Z) + 2 * z + row % 2


def load_messages(ref):
    parts = [ref[:, :, LANES * v : LANES * (v + 1)] for v in range(PAIRS)]
    return jnp.concatenate([p.reshape(2 * N_Z, LANES) for p in parts], axis=0)


def store_messages(ref, rows):
    for v in range(PAIRS):
        part = rows[2 * N_Z * v : 2 * N_Z * (v + 1)].reshape(N_Z, 2, LANES)
        ref[:, :, LANES * v : LANES * (v + 1)] = part.astype(BF16)


def slot_rows(ids):
    one_hot = (iota((N_EXPERT, TOK), 0) == ids).astype(F32)
    before = (iota((TOK, TOK), 0) < iota((TOK, TOK), 1)).astype(F32).astype(BF16)
    earlier = jnp.dot(one_hot.astype(BF16), before, preferred_element_type=F32)
    position = jnp.sum(earlier * one_hot, axis=0, keepdims=True).astype(I32)
    second = position >= HALF
    spot = jnp.where(second, position - HALF, position)
    upper = jnp.where(second, 1, 0)
    to_z, yl = ids // N_YL, ids % N_YL
    first = 6 * (2 * yl + upper)
    last = spot == HALF - 1
    group = jnp.where(last, 2 * upper + lax.axis_index("z") // 8, spot)
    tail = jnp.where(last, 24 + yl, first + 5)
    return flat_row(first + spot, to_z), flat_row(tail, to_z), group


def slot_map(row_main, row_tail):
    at = iota((FLAT, TOK), 0)
    main = (at == row_main).astype(F32).astype(BF16)
    tail = (at == row_tail).astype(F32).astype(BF16)
    return jnp.concatenate([main, tail], axis=1)


def dispatch_kernel(tok_hbm, logit_hbm, ids_hbm, out_ref, aux_ref, tok_ref, logit_ref, ids_ref, sems):
    copies = [
        pltpu.make_async_copy(src, dst, sems.at[i])
        for i, (src, dst) in enumerate(
            ((ids_hbm, ids_ref), (logit_hbm, logit_ref), (tok_hbm, tok_ref))
        )
    ]
    for copy in copies:
        copy.start()
    copies[0].wait()
    row_main, row_tail, group = slot_rows(ids_ref[...])
    aux_ref[0:1, :] = row_main
    aux_ref[1:2, :] = row_tail
    aux_ref[2:3, :] = group
    aux_ref[3:8, :] = jnp.zeros((5, TOK), I32)
    copies[1].wait()
    copies[2].wait()
    factor = jax.nn.sigmoid(logit_ref[...])
    scaled = (tok_ref[...].astype(F32) * factor).astype(BF16)
    tails = jnp.concatenate([scaled[LANES:, :].astype(F32)] * 4, axis=0)
    tails = jnp.where(iota((LANES, TOK), 0) // TAIL == group, tails, 0.0).astype(BF16)
    both = jnp.concatenate([scaled[:LANES, :], tails], axis=1)
    out = lax.dot_general(
        slot_map(row_main, row_tail), both, (((1,), (1,)), ((), ())), preferred_element_type=F32
    )
    store_messages(out_ref, out)


def weights_kernel(gate_hbm, up_hbm, down_hbm, out_ref, down_ref, sems):
    down_copy = pltpu.make_async_copy(down_hbm, down_ref, sems.at[2])
    down_copy.start()
    copies = [
        pltpu.make_async_copy(hbm.at[0], out_ref.at[i], sems.at[i])
        for i, hbm in enumerate((gate_hbm, up_hbm))
    ]
    for copy in copies:
        copy.start()
    down_copy.wait()
    for m in range(N_PART):
        k = m % 4
        at = WIDTH * m - TAIL * k
        window = down_ref[0, :, at : at + LANES]
        if k:
            low = down_ref[0, :, at + LANES : at + 2 * LANES].astype(F32)
            mixed = jnp.where(iota((FF, LANES), 1) >= TAIL * k, window.astype(F32), low)
            window = pltpu.roll(mixed, LANES - TAIL * k, 1).astype(BF16)
        rows, cols = FF * (m // 2), LANES * (m % 2)
        out_ref[2, rows : rows + FF, cols : cols + LANES] = window
    for g in range(4):
        lanes = iota((FF, LANES), 1) // TAIL
        total = jnp.zeros((FF, LANES), F32)
        for k in range(4):
            at = 4 * WIDTH * g + LANES * (k + 1)
            total = jnp.where(lanes == k, down_ref[0, :, at : at + LANES].astype(F32), total)
        rows, cols = FF * (8 + g // 2), LANES * (g % 2)
        out_ref[2, rows : rows + FF, cols : cols + LANES] = total.astype(BF16)
    for copy in copies:
        copy.wait()


MAIN = 6 * N_Z


def main_row(flat):
    return (flat // (2 * N_Z) * 2 + flat % 2) * N_Z + flat % (2 * N_Z) // 2


def last_row(flat):
    return flat % 2 * 8 + flat // 2 % 8


def select(rows, cols):
    return (rows == cols).astype(F32).astype(BF16)


def spread_kernel(in_ref, out_ref):
    flat = load_messages(in_ref)
    move = select(iota((MAIN, MAIN), 0), main_row(iota((1, MAIN), 1)))
    last = select(iota((16, 2 * N_Z), 0), last_row(iota((1, 2 * N_Z), 1)))
    ends = jnp.dot(last, flat[2 * N_YL * MAIN :], preferred_element_type=F32)
    for part in range(2 * N_YL):
        yl, h = part // 2, part % 2
        rows = flat[MAIN * part : MAIN * (part + 1)]
        block = jnp.dot(move, rows, preferred_element_type=F32)
        end = ends[8 * yl : 8 * (yl + 1)]
        if h:
            end = pltpu.roll(end, LANES // 2, 1)
        block = jnp.concatenate([block, end], axis=0).astype(BF16)
        for chip in range(N_CHIP):
            out_ref[place(yl, 2 * chip + h)] = block


def hidden_units(x_ref, weights):
    halves = []
    for w_ref in weights:
        total = jnp.zeros((ROWS, FF), F32)
        for n in range(MODEL // FF):
            if n < 8:
                starts, size = [WIDTH * m for m in (2 * n, 2 * n + 1)], LANES
            else:
                starts, size = [WIDTH * m + LANES for m in range(8 * n - 64, 8 * n - 56)], TAIL
            rows = jnp.concatenate([w_ref[at : at + size, :] for at in starts], axis=0)
            x = x_ref[:, FF * n : FF * (n + 1)]
            total = total + jnp.dot(x, rows, preferred_element_type=F32)
        halves.append(total)
    gate, up = halves
    return (gate / (1.0 + jnp.exp(-gate)) * up).astype(BF16)


def expert_kernel(
    x_ref, gate_ref, up_ref, own_down_ref, other_hbm, out_ref, other_ref, x_all, total, plain, sems
):
    copies = [pltpu.make_async_copy(other_hbm.at[i], other_ref.at[i], sems.at[i]) for i in range(3)]
    for i in (0, 1):
        copies[i].start()
    lanes = iota((N_Z, LANES), 1) // TAIL

    def turn(x, groups):
        shift = (TAIL * groups) % LANES
        return pltpu.roll(x, shift, 1) if shift else x

    def pick(parts):
        whole = jnp.zeros(parts[0].shape, F32)
        for k, part in enumerate(parts):
            whole = jnp.where(lanes[0 : part.shape[0]] == k, part, whole)
        return whole

    for yl in range(N_YL):
        for m in range(N_PART):
            x_all[PART * yl : PART * (yl + 1), LANES * m : LANES * (m + 1)] = x_ref[
                place(yl, m), 0:PART, :
            ]
        for g in range(4):
            parts = [place(yl, 4 * g + k) for k in range(4)]
            packed = [x_ref[i, PART : PART + N_Z, :].astype(F32) for i in parts]
            ends = [x_ref[i, PART + N_Z : BLOCK, :].astype(F32) for i in parts]
            cols = slice(N_PART * LANES + LANES * g, N_PART * LANES + LANES * (g + 1))
            made = [pick([turn(packed[k], k - p) for k in range(4)]) for p in range(4)]
            made += [pick([turn(ends[k], k - j) for k in range(4)]) for j in range(2)]
            x_all[PART * yl : PART * (yl + 1), cols] = jnp.concatenate(made, axis=0).astype(BF16)

    copies[2].start()
    own = hidden_units(x_all, (gate_ref.at[0], up_ref.at[0]))
    for i in range(10):
        cols = slice(FF * i, FF * (i + 1))
        plain[:, cols] = jnp.dot(own, own_down_ref[0, :, cols], preferred_element_type=F32)
    groups = iota((ROWS, LANES), 1) // TAIL
    for g in range(4):
        ends = jnp.zeros((ROWS, LANES), F32)
        for k in range(4):
            at, m = 4 * WIDTH * g + LANES * k, 4 * g + k
            low, high = plain[:, at : at + LANES], plain[:, at + LANES : at + 2 * LANES]
            ends = jnp.where(groups == k, high, ends)
            total[:, LANES * m : LANES * (m + 1)] = turn(jnp.where(groups >= k, low, high), -k)
        first = N_PART * LANES + LANES * g
        total[:, first : first + LANES] = ends
    copies[0].wait()
    copies[1].wait()
    other = hidden_units(x_all, (other_ref.at[0], other_ref.at[1]))
    copies[2].wait()

    def chunk(i):
        rows = slice(FF * i, FF * (i + 1))
        part = jnp.dot(other, other_ref[2, rows], preferred_element_type=F32)
        return total[:, rows] + part

    for i in (8, 9):
        total[:, FF * i : FF * (i + 1)] = chunk(i)
    for yl in range(N_YL):
        for g in range(4):
            cols = slice(N_PART * LANES + LANES * g, N_PART * LANES + LANES * (g + 1))
            main = [total[PART * yl + N_Z * p : PART * yl + N_Z * (p + 1), cols] for p in range(4)]
            first = PART * yl + 4 * N_Z
            ends = [total[first + 8 * j : first + 8 * (j + 1), cols] for j in range(2)]
            for k in range(4):
                made = [pick([turn(main[p], p - k) for p in range(4)])]
                made.append(pick([turn(ends[j], j - k) for j in range(2)]))
                rest = jnp.concatenate(made, axis=0).astype(BF16)
                out_ref[place(yl, 4 * g + k), PART:BLOCK, :] = rest
    for i in range(8):
        part = chunk(i).astype(BF16)
        for yl in range(N_YL):
            rows = slice(PART * yl, PART * (yl + 1))
            out_ref[place(yl, 2 * i), 0:PART, :] = part[rows, 0:LANES]
            out_ref[place(yl, 2 * i + 1), 0:PART, :] = part[rows, LANES:]


def reduce_kernel(in_ref, out_ref):
    move = select(iota((MAIN, MAIN), 1), main_row(iota((MAIN, 1), 0)))
    last = select(iota((2 * N_Z, 16), 1), last_row(iota((2 * N_Z, 1), 0)))
    moved, ends = [], []
    for part in range(2 * N_YL):
        yl, h = part // 2, part % 2
        total = in_ref[place(yl, h)].astype(F32)
        for chip in range(1, N_CHIP):
            total = total + in_ref[place(yl, 2 * chip + h)].astype(F32)
        rows = total[:MAIN].astype(BF16)
        moved.append(jnp.dot(move, rows, preferred_element_type=F32))
        if h:
            ends[yl] = ends[yl] + pltpu.roll(total[MAIN:], LANES // 2, 1)
        else:
            ends.append(total[MAIN:])
    ends = jnp.concatenate(ends, axis=0).astype(BF16)
    moved.append(jnp.dot(last, ends, preferred_element_type=F32))
    store_messages(out_ref, jnp.concatenate(moved, axis=0))


def combine_kernel(in_ref, aux_ref, out_ref):
    row_main, row_tail, group = aux_ref[0:1, :], aux_ref[1:2, :], aux_ref[2:3, :]
    flat = load_messages(in_ref)
    got = lax.dot_general(
        flat, slot_map(row_main, row_tail), (((0,), (0,)), ((), ())), preferred_element_type=F32
    )
    out_ref[0:LANES, :] = got[:, :TOK].astype(BF16)
    tails = jnp.where(iota((LANES, TOK), 0) // TAIL == group, got[:, TOK:], 0.0)
    tail = tails[0:TAIL] + tails[TAIL : 2 * TAIL] + tails[2 * TAIL : 3 * TAIL] + tails[3 * TAIL :]
    out_ref[LANES:WIDTH, :] = tail.astype(BF16)


def call(kernel, name, out, args, mib=16, scratch=(), flops=0, moved=1 << 20, spaces=pltpu.VMEM):
    spaces = spaces if isinstance(spaces, tuple) else (spaces,) * len(args)
    args = [
        pltpu.with_memory_space_constraint(x, space) if space is pltpu.HBM else x
        for x, space in zip(args, spaces)
    ]
    return pl.pallas_call(
        kernel,
        out_shape=out,
        in_specs=[pl.BlockSpec(memory_space=space) for space in spaces],
        scratch_shapes=list(scratch),
        compiler_params=pltpu.CompilerParams(vmem_limit_bytes=mib << 20),
        cost_estimate=pl.CostEstimate(flops=flops, bytes_accessed=moved, transcendentals=0),
        name=name,
    )(*args)


def exchange(x, axes):
    return lax.all_to_all(x, axes, 0, 0, tiled=True)


def on_device(tokens, route_logit, expert_ids, w_gate, w_up, w_down):
    shape = jax.ShapeDtypeStruct
    message = shape((N_Z, 2, PAIRS * LANES), BF16)
    blocks = shape((N_YL * N_PART, BLOCK, LANES), BF16)
    sent, aux = call(
        dispatch_kernel, "dispatch", (message, shape((8, TOK), I32)),
        (tokens.T, route_logit.reshape(1, TOK), expert_ids.reshape(1, TOK)),
        spaces=pltpu.HBM,
        scratch=(
            pltpu.VMEM((WIDTH, TOK), BF16), pltpu.VMEM((1, TOK), F32), pltpu.VMEM((1, TOK), I32),
            pltpu.SemaphoreType.DMA((3,)),
        ),
    )
    arrived = exchange(sent, "z")
    own = call(
        weights_kernel, "weights", shape((3, MODEL, FF), BF16), (w_gate, w_up, w_down),
        mib=32, moved=8 << 20, spaces=pltpu.HBM,
        scratch=(pltpu.VMEM((1, FF, MODEL), BF16), pltpu.SemaphoreType.DMA((3,))),
    )
    other = lax.ppermute(own, "core", [(0, 1), (1, 0)])
    pieces = exchange(call(spread_kernel, "spread", blocks, (arrived,), flops=50_000_000_000), PLANE)
    partial = call(
        expert_kernel, "expert", blocks, (pieces, w_gate, w_up, w_down, other), mib=20,
        spaces=(pltpu.VMEM,) * 4 + (pltpu.HBM,),
        scratch=(
            pltpu.VMEM((3, MODEL, FF), BF16), pltpu.VMEM((ROWS, MODEL), BF16),
            pltpu.VMEM((ROWS, MODEL), F32), pltpu.VMEM((ROWS, MODEL), F32),
            pltpu.SemaphoreType.DMA((3,)),
        ),
        flops=12 * ROWS * MODEL * FF, moved=8 << 20,
    )
    terms = exchange(partial, PLANE)
    back = call(reduce_kernel, "reduce", message, (terms,))
    returned = exchange(back, "z")
    mixed = call(combine_kernel, "combine", shape((WIDTH, TOK), BF16), (returned, aux))
    return mixed.T


def solution(mesh):
    fine = Mesh(mesh.devices.reshape(16, 2, 2, 4, 2), EXPERT + TENSOR)
    return jax.shard_map(
        on_device,
        mesh=fine,
        in_specs=(
            P(EXPERT, TENSOR),
            P(EXPERT),
            P(EXPERT, None),
            P(EXPERT, None, TENSOR),
            P(EXPERT, None, TENSOR),
            P(EXPERT, TENSOR, None),
        ),
        out_specs=P(EXPERT, TENSOR),
        check_vma=False,
    )
```

```python
import jax
import jax.numpy as jnp
from jax import lax
from jax.experimental import pallas as pl
from jax.experimental.pallas import tpu as pltpu
from jax.sharding import Mesh, PartitionSpec as P

EXPERT = ("z", "yl")
TENSOR = ("yh", "x", "core")
PLANE = ("yl",) + TENSOR
BF16, F32, I32 = jnp.bfloat16, jnp.float32, jnp.int32

N_Z, N_YL, N_PART, N_CHIP = 16, 2, 16, 8
N_EXPERT = N_Z * N_YL
TOK, WIDTH, FF = 256, 160, 256
MODEL = N_PART * WIDTH
HALF = 5
PART = N_Z * HALF
ROWS = N_YL * PART
LANES, TAIL = 128, WIDTH - 128
BLOCK = PART + N_Z + 8
PAIRS = 13
FLAT = PAIRS * N_Z * 2


def iota(shape, axis):
    return lax.broadcasted_iota(I32, shape, axis)


def flat_row(row, z):
    return row // 2 * (2 * N_Z) + 2 * z + row % 2


def load_messages(ref):
    parts = [ref[:, :, LANES * v : LANES * (v + 1)] for v in range(PAIRS)]
    return jnp.concatenate([p.reshape(2 * N_Z, LANES) for p in parts], axis=0)


def store_messages(ref, rows):
    for v in range(PAIRS):
        part = rows[2 * N_Z * v : 2 * N_Z * (v + 1)].reshape(N_Z, 2, LANES)
        ref[:, :, LANES * v : LANES * (v + 1)] = part.astype(BF16)


def slot_rows(ids):
    one_hot = (iota((N_EXPERT, TOK), 0) == ids).astype(F32)
    before = (iota((TOK, TOK), 0) < iota((TOK, TOK), 1)).astype(F32).astype(BF16)
    earlier = jnp.dot(one_hot.astype(BF16), before, preferred_element_type=F32)
    position = jnp.sum(earlier * one_hot, axis=0, keepdims=True).astype(I32)
    second = position >= HALF
    place = jnp.where(second, position - HALF, position)
    upper = jnp.where(second, 1, 0)
    to_z, yl = ids // N_YL, ids % N_YL
    first = 6 * (2 * yl + upper)
    last = place == HALF - 1
    group = jnp.where(last, 2 * upper + lax.axis_index("z") // 8, place)
    tail = jnp.where(last, 24 + yl, first + 5)
    return flat_row(first + place, to_z), flat_row(tail, to_z), group


def slot_map(row_main, row_tail):
    at = iota((FLAT, TOK), 0)
    main = (at == row_main).astype(F32).astype(BF16)
    tail = (at == row_tail).astype(F32).astype(BF16)
    return jnp.concatenate([main, tail], axis=1)


def dispatch_kernel(
    tok_hbm, logit_hbm, ids_hbm, gate_hbm, up_hbm, down_hbm, out_ref, aux_ref, own_ref,
    tok_ref, logit_ref, ids_ref, down_ref, sems,
):
    first = ((ids_hbm, ids_ref), (logit_hbm, logit_ref), (tok_hbm, tok_ref), (down_hbm, down_ref))
    loads = [pltpu.make_async_copy(src, dst, sems.at[i]) for i, (src, dst) in enumerate(first)]
    for load in loads:
        load.start()
    copies = [
        pltpu.make_async_copy(hbm.at[0], own_ref.at[i], sems.at[4 + i])
        for i, hbm in enumerate((gate_hbm, up_hbm))
    ]
    for copy in copies:
        copy.start()
    loads[0].wait()
    row_main, row_tail, group = slot_rows(ids_ref[...])
    aux_ref[0:1, :] = row_main
    aux_ref[1:2, :] = row_tail
    aux_ref[2:3, :] = group
    aux_ref[3:8, :] = jnp.zeros((5, TOK), I32)
    moves = slot_map(row_main, row_tail)
    loads[1].wait()
    loads[2].wait()
    factor = jax.nn.sigmoid(logit_ref[...])
    scaled = (tok_ref[...].astype(F32) * factor).astype(BF16)
    tails = jnp.concatenate([scaled[LANES:, :].astype(F32)] * 4, axis=0)
    tails = jnp.where(iota((LANES, TOK), 0) // TAIL == group, tails, 0.0).astype(BF16)
    both = jnp.concatenate([scaled[:LANES, :], tails], axis=1)
    out = lax.dot_general(moves, both, (((1,), (1,)), ((), ())), preferred_element_type=F32)
    store_messages(out_ref, out)

    loads[3].wait()
    for m in range(N_PART):
        k = m % 4
        at = WIDTH * m - TAIL * k
        window = down_ref[0, :, at : at + LANES]
        if k:
            low = down_ref[0, :, at + LANES : at + 2 * LANES].astype(F32)
            mixed = jnp.where(iota((FF, LANES), 1) >= TAIL * k, window.astype(F32), low)
            window = pltpu.roll(mixed, LANES - TAIL * k, 1).astype(BF16)
        rows, cols = FF * (m // 2), LANES * (m % 2)
        own_ref[2, rows : rows + FF, cols : cols + LANES] = window
    lanes = iota((FF, LANES), 1) // TAIL
    for g in range(4):
        total = jnp.zeros((FF, LANES), F32)
        for k in range(4):
            at = 4 * WIDTH * g + LANES * (k + 1)
            total = jnp.where(lanes == k, down_ref[0, :, at : at + LANES].astype(F32), total)
        rows, cols = FF * (8 + g // 2), LANES * (g % 2)
        own_ref[2, rows : rows + FF, cols : cols + LANES] = total.astype(BF16)
    for copy in copies:
        copy.wait()


MAIN = 6 * N_Z


def main_row(flat):
    return (flat // (2 * N_Z) * 2 + flat % 2) * N_Z + flat % (2 * N_Z) // 2


def last_row(flat):
    return flat % 2 * 8 + flat // 2 % 8


def select(rows, cols):
    return (rows == cols).astype(F32).astype(BF16)


def spread_kernel(in_ref, out_ref):
    flat = load_messages(in_ref)
    move = select(iota((MAIN, MAIN), 0), main_row(iota((1, MAIN), 1)))
    last = select(iota((16, 2 * N_Z), 0), last_row(iota((1, 2 * N_Z), 1)))
    ends = jnp.dot(last, flat[2 * N_YL * MAIN :], preferred_element_type=F32)
    for part in range(2 * N_YL):
        yl, h = part // 2, part % 2
        rows = flat[MAIN * part : MAIN * (part + 1)]
        block = jnp.dot(move, rows, preferred_element_type=F32)
        end = ends[8 * yl : 8 * (yl + 1)]
        if h:
            end = pltpu.roll(end, LANES // 2, 1)
        block = jnp.concatenate([block, end], axis=0).astype(BF16)
        for chip in range(N_CHIP):
            out_ref[N_PART * yl + 2 * chip + h] = block


def hidden_units(x_ref, w_ref):
    halves = []
    for i in range(2):
        total = jnp.zeros((ROWS, FF), F32)
        for n in range(MODEL // FF):
            if n < 8:
                starts, size = [WIDTH * m for m in (2 * n, 2 * n + 1)], LANES
            else:
                starts, size = [WIDTH * m + LANES for m in range(8 * n - 64, 8 * n - 56)], TAIL
            rows = jnp.concatenate([w_ref[i, at : at + size] for at in starts], axis=0)
            x = x_ref[:, FF * n : FF * (n + 1)]
            total = total + jnp.dot(x, rows, preferred_element_type=F32)
        halves.append(total)
    gate, up = halves
    return (gate / (1.0 + jnp.exp(-gate)) * up).astype(BF16)


def expert_kernel(x_ref, own_ref, other_ref, out_ref, x_all, total):
    lanes = iota((N_Z, LANES), 1) // TAIL

    def turn(x, groups):
        shift = (TAIL * groups) % LANES
        return pltpu.roll(x, shift, 1) if shift else x

    def pick(parts):
        whole = jnp.zeros(parts[0].shape, F32)
        for k, part in enumerate(parts):
            whole = jnp.where(lanes[0 : part.shape[0]] == k, part, whole)
        return whole

    for yl in range(N_YL):
        for m in range(N_PART):
            x_all[PART * yl : PART * (yl + 1), LANES * m : LANES * (m + 1)] = x_ref[
                N_PART * yl + m, 0:PART, :
            ]
        for g in range(4):
            parts = [N_PART * yl + 4 * g + k for k in range(4)]
            packed = [x_ref[i, PART : PART + N_Z, :].astype(F32) for i in parts]
            ends = [x_ref[i, PART + N_Z : BLOCK, :].astype(F32) for i in parts]
            cols = slice(N_PART * LANES + LANES * g, N_PART * LANES + LANES * (g + 1))
            made = [pick([turn(packed[k], k - p) for k in range(4)]) for p in range(4)]
            made += [pick([turn(ends[k], k - j) for k in range(4)]) for j in range(2)]
            x_all[PART * yl : PART * (yl + 1), cols] = jnp.concatenate(made, axis=0).astype(BF16)

    def down(hidden, w_ref, i):
        return jnp.dot(hidden, w_ref[2, FF * i : FF * (i + 1)], preferred_element_type=F32)

    own = hidden_units(x_all, own_ref)
    other = hidden_units(x_all, other_ref)

    def chunk(i):
        return down(own, own_ref, i) + down(other, other_ref, i)

    for i in (8, 9):
        total[:, FF * (i - 8) : FF * (i - 7)] = chunk(i)
    for yl in range(N_YL):
        for g in range(4):
            cols = slice(LANES * g, LANES * (g + 1))
            main = [total[PART * yl + N_Z * p : PART * yl + N_Z * (p + 1), cols] for p in range(4)]
            first = PART * yl + 4 * N_Z
            ends = [total[first + 8 * j : first + 8 * (j + 1), cols] for j in range(2)]
            for k in range(4):
                made = [pick([turn(main[p], p - k) for p in range(4)])]
                made.append(pick([turn(ends[j], j - k) for j in range(2)]))
                rest = jnp.concatenate(made, axis=0).astype(BF16)
                out_ref[N_PART * yl + 4 * g + k, PART:BLOCK, :] = rest
    for i in range(8):
        part = chunk(i).astype(BF16)
        for yl in range(N_YL):
            rows = slice(PART * yl, PART * (yl + 1))
            out_ref[N_PART * yl + 2 * i, 0:PART, :] = part[rows, 0:LANES]
            out_ref[N_PART * yl + 2 * i + 1, 0:PART, :] = part[rows, LANES:]


def reduce_kernel(in_ref, out_ref):
    move = select(iota((MAIN, MAIN), 1), main_row(iota((MAIN, 1), 0)))
    last = select(iota((2 * N_Z, 16), 1), last_row(iota((2 * N_Z, 1), 0)))
    moved, ends = [], []
    for part in range(2 * N_YL):
        yl, h = part // 2, part % 2
        total = in_ref[N_PART * yl + h].astype(F32)
        for chip in range(1, N_CHIP):
            total = total + in_ref[N_PART * yl + 2 * chip + h].astype(F32)
        rows = total[:MAIN].astype(BF16)
        moved.append(jnp.dot(move, rows, preferred_element_type=F32))
        if h:
            ends[yl] = ends[yl] + pltpu.roll(total[MAIN:], LANES // 2, 1)
        else:
            ends.append(total[MAIN:])
    ends = jnp.concatenate(ends, axis=0).astype(BF16)
    moved.append(jnp.dot(last, ends, preferred_element_type=F32))
    store_messages(out_ref, jnp.concatenate(moved, axis=0))


def combine_kernel(in_ref, aux_ref, out_ref):
    row_main, row_tail, group = aux_ref[0:1, :], aux_ref[1:2, :], aux_ref[2:3, :]
    flat = load_messages(in_ref)
    got = lax.dot_general(
        flat, slot_map(row_main, row_tail), (((0,), (0,)), ((), ())), preferred_element_type=F32
    )
    out_ref[0:LANES, :] = got[:, :TOK].astype(BF16)
    tails = jnp.where(iota((LANES, TOK), 0) // TAIL == group, got[:, TOK:], 0.0)
    tail = tails[0:TAIL] + tails[TAIL : 2 * TAIL] + tails[2 * TAIL : 3 * TAIL] + tails[3 * TAIL :]
    out_ref[LANES:WIDTH, :] = tail.astype(BF16)


def call(kernel, name, out, args, mib=16, scratch=(), flops=0, moved=1 << 20, spaces=pltpu.VMEM):
    spaces = spaces if isinstance(spaces, tuple) else (spaces,) * len(args)
    args = [
        pltpu.with_memory_space_constraint(x, space) if space is pltpu.HBM else x
        for x, space in zip(args, spaces)
    ]
    return pl.pallas_call(
        kernel,
        out_shape=out,
        in_specs=[pl.BlockSpec(memory_space=space) for space in spaces],
        scratch_shapes=list(scratch),
        compiler_params=pltpu.CompilerParams(vmem_limit_bytes=mib << 20),
        cost_estimate=pl.CostEstimate(flops=flops, bytes_accessed=moved, transcendentals=0),
        name=name,
    )(*args)


def exchange(x, axes):
    return lax.all_to_all(x, axes, 0, 0, tiled=True)


def on_device(tokens, route_logit, expert_ids, w_gate, w_up, w_down):
    shape = jax.ShapeDtypeStruct
    message = shape((N_Z, 2, PAIRS * LANES), BF16)
    blocks = shape((N_YL * N_PART, BLOCK, LANES), BF16)
    weights = shape((3, MODEL, FF), BF16)
    sent, aux, own = call(
        dispatch_kernel, "dispatch", (message, shape((8, TOK), I32), weights),
        (
            tokens.T, route_logit.reshape(1, TOK), expert_ids.reshape(1, TOK),
            w_gate, w_up, w_down,
        ),
        spaces=pltpu.HBM, moved=8 << 20,
        scratch=(
            pltpu.VMEM((WIDTH, TOK), BF16), pltpu.VMEM((1, TOK), F32), pltpu.VMEM((1, TOK), I32),
            pltpu.VMEM((1, FF, MODEL), BF16),
            pltpu.SemaphoreType.DMA((6,)),
        ),
    )
    other = lax.ppermute(own, "core", [(0, 1), (1, 0)])
    arrived = exchange(sent, "z")
    pieces = exchange(call(spread_kernel, "spread", blocks, (arrived,)), PLANE)
    partial = call(
        expert_kernel, "expert", blocks, (pieces, own, other), mib=32,
        scratch=(pltpu.VMEM((ROWS, MODEL), BF16), pltpu.VMEM((ROWS, 4 * LANES), F32)),
        flops=12 * ROWS * MODEL * FF, moved=8 << 20,
    )
    terms = exchange(partial, PLANE)
    back = call(reduce_kernel, "reduce", message, (terms,))
    returned = exchange(back, "z")
    mixed = call(combine_kernel, "combine", shape((WIDTH, TOK), BF16), (returned, aux))
    return mixed.T


def solution(mesh):
    fine = Mesh(mesh.devices.reshape(16, 2, 2, 4, 2), EXPERT + TENSOR)
    return jax.shard_map(
        on_device,
        mesh=fine,
        in_specs=(
            P(EXPERT, TENSOR),
            P(EXPERT),
            P(EXPERT, None),
            P(EXPERT, None, TENSOR),
            P(EXPERT, None, TENSOR),
            P(EXPERT, TENSOR, None),
        ),
        out_specs=P(EXPERT, TENSOR),
        check_vma=False,
    )
```
